256 devices in a mesh: grp: 4 (over x), orb: 64 (over z, y, core).
Axes of the slice: x: 4, y: 4, z: 8, core: 2. Of those that a mesh axis runs over, the one named last changes fastest.
Arguments:
- wavevectors: float32 [3, 1024], replicated, may hold values from -3 to 3
- coefficients: bfloat16 [2048, 1024], P(None, 'orb'), may hold values from -0.0017089844 to 0.0017089844
- inverse: float32 [256, 1024, 1024], P(('grp', 'orb')), may hold values from -0.5 to 0.5
- positions: float32 [256, 3, 1024], P(('grp', 'orb')), may hold values from 0 to 10
- displacements: float32 [2, 256, 3, 16], P(None, ('grp', 'orb')), may hold values from -0.3125 to 0.3125
- moved: int32 [2, 256, 16], P(None, ('grp', 'orb')), may hold values from 0 to 1023, as said below
- donor: int32 [64], P('orb'), may hold values from 0 to 3
- take: int32 [256], P(('grp', 'orb')), may hold values 0 or 1
- log_weight: float32 [256], P(('grp', 'orb')), may hold values from -1 to 1
Outputs:
- new_inverse: float32 [256, 1024, 1024], P(('grp', 'orb'))
- drift: float32 [2, 256, 3, 16], P(None, ('grp', 'orb'))
- laplacian: float32 [2, 256, 16], P(None, ('grp', 'orb'))
- new_weight: float32 [256], P(('grp', 'orb'))
The draws below stay inside these ranges and needn't reach their ends.
Inputs may be any that keep to these rules, and one draw needn't show every extreme that they name: `moved`: within a walker slot the 32 entries are distinct electrons.
All inputs are finite; a program needn't handle non-finite values. No bound on the sum of `take` on one device may be relied on, other than what follows from the above.
Results may differ from the reference program's by a relative error of at most 0.004.
Values may be sent and summed in bfloat16 or wider, within the bound.
A program may use at most 64 MiB of HBM per device.

```python
import jax
import jax.numpy as jnp
from jax import lax

NE = 1024
NPW = 2048
K = 16
UPD = 2
NG = 1024
W = 256
N_GRP = 4
N_ORB = 64


def draw_moved(key, part):
    keys = jax.random.split(jax.random.fold_in(key, 17), W)

    def pick(walker_key):
        return jax.random.permutation(walker_key, NE)[:UPD * K]
    rows = jax.vmap(pick)(keys)
    return rows.reshape(W, UPD, K).transpose(1, 0, 2).astype(jnp.int32)


def place_ends(array, rng, low, high):
    longest = array.shape.index(max(array.shape))
    spots = []
    for shift in (0, 1):
        where = [jax.random.randint(jax.random.fold_in(rng, axis), (), 0, length) for axis, length in enumerate(array.shape)]
        where[longest] = (where[longest] + shift) % array.shape[longest]
        spots.append(tuple(where))
    return array.at[spots[0]].set(low).at[spots[1]].set(high)


def levels(key, extent, pieces, smallest, largest):
    def one(dim, blocks):
        draws = jax.random.uniform(jax.random.fold_in(jax.random.fold_in(key, 6), dim), (blocks,), jnp.float32, smallest / len(pieces), largest / len(pieces))
        return jnp.repeat(jnp.exp(draws), extent[dim] // blocks).reshape((-1,) + (1,) * (len(extent) - dim - 1))

    loudness = one(*pieces[0])
    for cut in pieces[1:]:
        loudness = loudness * one(*cut)
    return loudness


def scatter_about(stream_key, dims, scale, bound, cuts=(), held_as=jnp.bfloat16):
    level = levels(stream_key, dims, cuts, -0.22, 0.18) if cuts else 1.0
    array = jax.random.normal(stream_key, dims, jnp.float32) * scale * level
    return jnp.minimum(jnp.maximum(array, -bound), bound).astype(held_as)


def setup_inputs(seed: int = 0) -> dict:
    seeds = jax.random.split(jax.random.key(seed), 10)
    return {
        "wavevectors": jnp.clip(jax.random.uniform(seeds[0], (3, NG), jnp.float32, -3.0, 3.0), -3.0, 3.0),
        "coefficients": scatter_about(seeds[1], (NPW, NE), 0.0003, 0.0017089844, ((1, 64),)),
        "inverse": jnp.clip(jax.random.uniform(seeds[2], (W, NE, NE), jnp.float32, -0.5, 0.5) * levels(seeds[2], (W, NE, NE), ((0, 256),), -0.4, 0.0), -0.5, 0.5),
        "positions": jnp.clip(10.0 * jax.random.uniform(seeds[3], (W, 3, NE), jnp.float32) ** levels(seeds[3], (W, 3, NE), ((0, 256),), -0.2, 0.2), 0.0, 10.0),
        "displacements": scatter_about(seeds[4], (UPD, W, 3, K), 0.05, 0.3125, ((1, 256),), jnp.float32),
        "moved": draw_moved(jax.random.fold_in(seeds[9], 71), 0),
        "donor": place_ends(jax.random.randint(seeds[6], (N_ORB,), 0, N_GRP), jax.random.fold_in(seeds[6], 1), 0, N_GRP - 1).astype(jnp.int32),
        "take": place_ends((jax.random.randint(seeds[7], (W,), 0, 2) < 1).astype(jnp.int32), jax.random.fold_in(seeds[7], 1), 0, 1),
        "log_weight": jnp.clip(jax.random.uniform(seeds[8], (W,), jnp.float32, -1.0, 1.0) * levels(seeds[8], (W,), ((0, 256),), -0.4, 0.0), -1.0, 1.0),
    }


precise = lax.Precision.HIGHEST

def build_tables(coefficients, wavevectors):
    coeff_f = coefficients.astype(jnp.float32)
    wave_count = wavevectors.shape[1]
    cos_part = coeff_f[:wave_count]
    sin_part = coeff_f[wave_count:]
    parts = [coeff_f]
    for component in range(3):
        scale = wavevectors[component][:, None]
        parts.append(jnp.concatenate([scale * sin_part, -scale * cos_part], 0))
    squared = wavevectors[0] * wavevectors[0] + wavevectors[1] * wavevectors[1] + wavevectors[2] * wavevectors[2]
    doubled = jnp.concatenate([squared, squared], 0)[:, None]
    parts.append(-doubled * coeff_f)
    return jnp.stack(parts, 1).astype(jnp.bfloat16)

def evaluate(points, wavevectors, coefficients, derived):
    count = points.shape[1] // 2
    phases = points[0][:, None] * wavevectors[0][None, :] + points[1][:, None] * wavevectors[1][None, :]
    phases = phases + points[2][:, None] * wavevectors[2][None, :]
    waves = jnp.concatenate([jnp.cos(phases), jnp.sin(phases)], 1).astype(jnp.bfloat16)
    before = jnp.dot(waves[:count].astype(jnp.float32), coefficients.astype(jnp.float32), preferred_element_type=jnp.float32)
    flat = derived.reshape(derived.shape[0], -1)
    after = jnp.dot(waves[count:].astype(jnp.float32), flat.astype(jnp.float32), preferred_element_type=jnp.float32).reshape(count, 5, -1)
    change = after[:, 0] - before
    return jnp.concatenate([change[:, None], after[:, 1:]], 1)

def woodbury(matrix, values, chosen):
    change = values[:, 0]
    columns = matrix[:, chosen]
    ratio_matrix = jnp.eye(change.shape[0], dtype=matrix.dtype) + jnp.dot(change, columns, precision=precise)
    product = jnp.dot(change, matrix, precision=precise)
    solved = jnp.linalg.solve(ratio_matrix, product)
    updated = matrix - jnp.dot(columns, solved, precision=precise)
    log_ratio = jnp.linalg.slogdet(ratio_matrix)[1]
    fresh_columns = updated[:, chosen]
    drift = jnp.einsum('kaj,jk->ak', values[:, 1:4], fresh_columns, precision=precise)
    laplacian = jnp.einsum('kj,jk->k', values[:, 4], fresh_columns, precision=precise)
    return (updated, log_ratio, drift, laplacian)

def reference(wavevectors, coefficients, inverse, positions, displacements, moved, donor, take, log_weight):
    derived = build_tables(coefficients, wavevectors)

    def advance(matrix, places, shifted, chosen):
        before_points = places[:, chosen]
        moved_to = before_points + shifted
        points = jnp.concatenate([before_points, moved_to], 1)
        values = evaluate(points, wavevectors, coefficients, derived)
        updated, log_ratio, drift, laplacian = woodbury(matrix, values, chosen)
        places = places.at[:, chosen].set(moved_to)
        return (updated, places, log_ratio, drift, laplacian)

    def first_pass(items):
        return advance(items[0], items[1], items[2], items[3])
    matrix_one, places_one, ratio_one, drift_one, lap_one = lax.map(first_pass, (inverse, positions, displacements[0], moved[0]))
    walker = jnp.arange(W, dtype=jnp.int32)
    group = walker // N_ORB
    column = walker % N_ORB
    source = donor[column]
    parent = jnp.where(jnp.logical_and(take == 1, group != source), source * N_ORB + column, walker).astype(jnp.int32)
    weight_one = log_weight + ratio_one

    def second_pass(items):
        return advance(matrix_one[items[0]], places_one[items[0]], items[1], items[2])
    matrix_two, places_two, ratio_two, drift_two, lap_two = lax.map(second_pass, (parent, displacements[1], moved[1]))
    final_weight = weight_one[parent] + ratio_two
    return (matrix_two, jnp.stack([drift_one, drift_two]), jnp.stack([lap_one, lap_two]), final_weight)
```

```python
import functools

import jax
import jax.numpy as jnp
from jax import lax
from jax.experimental import pallas as pl
from jax.experimental.pallas import tpu as pltpu
from jax.sharding import PartitionSpec as P

F32 = jnp.float32
BF16 = jnp.bfloat16
NX, NY, NZ = 4, 4, 8
LAG = 2
CHUNK = 32
K = 16
HIGH = lax.Precision.HIGHEST


def nn(a, b, precision=None):
    return lax.dot_general(
        a, b, (((1,), (0,)), ((), ())), precision=precision, preferred_element_type=F32
    )


def nt(a, b, precision=None):
    return lax.dot_general(
        a, b, (((1,), (1,)), ((), ())), precision=precision, preferred_element_type=F32
    )


def split(a):
    hi = a.astype(BF16)
    return hi, (a - hi.astype(F32)).astype(BF16)


def iota(shape, dim):
    return lax.broadcasted_iota(jnp.int32, shape, dim)


def column(row):
    return jnp.sum(jnp.where(iota((K, K), 0) == iota((K, K), 1), row, 0.0), 1, keepdims=True)


def one_hot(indices, width):
    return jnp.where(iota((K, width), 1) == indices.astype(jnp.int32), 1.0, 0.0)


def pick(hot, row):
    return jnp.sum(hot * row, 1, keepdims=True)


def invert(ratio):
    a = ratio
    lane = iota(a.shape, 2)
    row = iota((a.shape[0], K, 1), 1)
    pivots = jnp.ones((a.shape[0], 1, a.shape[2]), F32)
    for k in range(K):
        col = jnp.sum(jnp.where(lane == k, a, 0.0), 2, keepdims=True)
        size = jnp.where(row >= k, jnp.abs(col), -1.0)
        best = jnp.max(size, 1, keepdims=True)
        where = jnp.min(jnp.where(size == best, row, K), 1, keepdims=True)
        chosen = row == where
        pivot_row = jnp.sum(jnp.where(chosen, a, 0.0), 1, keepdims=True)
        pivot = jnp.sum(jnp.where(chosen, col, 0.0), 1, keepdims=True)
        other = jnp.where(chosen, a[:, k : k + 1], a)
        factor = jnp.where(chosen, col[:, k : k + 1], col)
        scaled = pivot_row / pivot
        a = jnp.where(row == k, scaled, other - factor * scaled)
        pivots = jnp.where(lane[:, :1] == k, pivot, pivots)
    logs = jnp.sum(jnp.log(jnp.abs(pivots)), 2, keepdims=True)
    return a[:, :, K : 2 * K], logs


def augmented(x):
    r, c = iota(x.shape, 0), iota(x.shape, 1)
    return x + jnp.where((c == r) | (c == r + K), 1.0, 0.0)


def wave_rows(points, kvec, with_slopes):
    phases = points[0] * kvec[0:1] + points[1] * kvec[1:2]
    phases = phases + points[2] * kvec[2:3]
    cos = jnp.cos(phases).astype(BF16)
    sin = jnp.sin(phases).astype(BF16)
    rows = [jnp.concatenate([cos, sin], 1)]
    if with_slopes:
        cos_f, sin_f = cos.astype(F32), sin.astype(F32)
        for a in range(3):
            k = kvec[a : a + 1]
            rows.append(jnp.concatenate([(-k * sin_f).astype(BF16), (k * cos_f).astype(BF16)], 1))
        square = kvec[0:1] * kvec[0:1] + kvec[1:2] * kvec[1:2] + kvec[2:3] * kvec[2:3]
        rows.append(
            jnp.concatenate([(-square * cos_f).astype(BF16), (-square * sin_f).astype(BF16)], 1)
        )
    return jnp.concatenate(rows, 0)


def diagonals(block):
    eye = iota((K, K), 0) == iota((K, K), 1)
    return [
        jnp.sum(jnp.where(eye, block[K * (i + 1) : K * (i + 2)], 0.0), 0, keepdims=True)
        for i in range(4)
    ]


def main_kernel(
    donor, take, log_weight, kvec, pos, disp, moved, coef, inverse,
    mhi, mlo, ccat, scat, drift, lap, weight,
    mf, cbuf, sxp, sxm, rxp, rxm, pk_pos, pk_small, waves, values, gath, amat,
    m_sem, c_sem, y_send, y_recv, p_send, p_recv, q_send, q_recv,
    xp_send, xp_recv, xm_send, xm_recv, zp_send, zp_recv, zm_send, zm_recv,
    so_send, so_recv, sp_send, sp_recv, sm_send, sm_recv,
):
    ne = mf.shape[0]
    steps = rxp.shape[0]
    chunks = ne // 2 // CHUNK
    g = lax.axis_index("grp")
    o = lax.axis_index("orb")
    core, y, z = lax.rem(o, 2), lax.rem(o // 2, NY), o // (2 * NY)
    zy = z * NY + y

    def orb(zz, yy, cc):
        return (zz * NY + yy) * 2 + cc

    def turn(value, by, size):
        return lax.rem(value + by + size, size)

    def remote(src, dst, send, recv, grp, orb_index):
        return pltpu.make_async_remote_copy(
            src_ref=src, dst_ref=dst, send_sem=send, recv_sem=recv,
            device_id=(grp, orb_index), device_id_type=pl.DeviceIdType.MESH,
        )

    matrix_copy = pltpu.make_async_copy(inverse.at[0], mf, m_sem)
    matrix_copy.start()
    own_shard = pltpu.make_async_copy(coef, cbuf.at[zy, core], c_sem)
    own_shard.start()

    moves = moved[...].astype(F32)
    small = jnp.zeros((K, 128), F32)
    lane = iota((K, 128), 1)
    columns = [column(moves[0])]
    columns += [column(disp[0, 0, a : a + 1]) for a in range(3)]
    columns.append(jnp.full((K, 1), log_weight[0], F32))
    for i, c in enumerate(columns):
        small = jnp.where(lane == i, c, small)
    pk_small[g] = small
    pk_pos[g] = pos[0]

    barrier = pltpu.get_barrier_semaphore()
    partners = [(turn(g, d, NX), o) for d in range(1, NX)]
    partners += [(g, orb(z, turn(y, d, NY), core)) for d in range(1, NY)]
    up, down = orb(turn(z, 1, NZ), y, core), orb(turn(z, -1, NZ), y, core)
    partners += [(g, up), (g, down)]
    sibling = orb(z, y, 1 - core)
    partners += [(g, sibling)]
    for partner in partners:
        pl.semaphore_signal(
            barrier, inc=1, device_id=partner, device_id_type=pl.DeviceIdType.MESH
        )
    pl.semaphore_wait(barrier, len(partners))

    y_copies = [
        remote(coef, cbuf.at[zy, core], y_send.at[d - 1], y_recv.at[d - 1], g,
               orb(z, turn(y, d, NY), core))
        for d in range(1, NY)
    ]
    packets = []
    for d in range(1, NX):
        to = turn(g, d, NX)
        packets.append(remote(pk_pos.at[g], pk_pos.at[g], p_send.at[d - 1], p_recv.at[d - 1], to, o))
        packets.append(
            remote(pk_small.at[g], pk_small.at[g], q_send.at[d - 1], q_recv.at[d - 1], to, o)
        )

    is_source = donor[0] == g
    right, left = turn(g, 1, NX), turn(g, -1, NX)
    matrix_copy.wait()
    x_copies = {}

    def x_step(t):
        if t >= LAG:
            for copy in x_copies[t - LAG]:
                copy.wait_recv()
        if t < chunks:
            for half, sent, got in ((0, sxp, rxp), (1, sxm, rxm)):
                first = half * (ne // 2) + t * CHUNK
                own = mf[first : first + CHUNK].astype(BF16)
                sent[t] = jnp.where(is_source, own, got[t - LAG]) if t >= LAG else own
            sources = (sxp.at[t], sxm.at[t])
        else:
            sources = (rxp.at[t - LAG], rxm.at[t - LAG])
        x_copies[t] = (
            remote(sources[0], rxp.at[t], xp_send.at[t], xp_recv.at[t], right, o),
            remote(sources[1], rxm.at[t], xm_send.at[t], xm_recv.at[t], left, o),
        )
        for copy in x_copies[t]:
            copy.start()

    z_moves = NZ - 1
    z_copies, sib_copies = {}, []

    def half_block(zz, half):
        return cbuf.at[pl.ds(zz * NY + half * (NY // 2), NY // 2), core]

    def to_sibling(ref, send, recv):
        copy = remote(ref, ref, send, recv, g, sibling)
        copy.start()
        sib_copies.append(copy)

    def arrived(k):
        for copy in z_copies[k]:
            copy.wait_recv()
        half = k % 2
        to_sibling(half_block(turn(z, -1 - k // 2, NZ), half), sp_send.at[k], sp_recv.at[k])
        to_sibling(half_block(turn(z, 1 + k // 2, NZ), 1 - half), sm_send.at[k], sm_recv.at[k])

    def z_step(k):
        if k == 0:
            own_shard.wait()
            for copy in y_copies:
                copy.wait_recv()
            for half in range(2):
                to_sibling(half_block(z, half), so_send.at[half], so_recv.at[half])
        if k >= 2:
            arrived(k - 2)
        half = k % 2
        ref_p = half_block(turn(z, -(k // 2), NZ), half)
        ref_m = half_block(turn(z, k // 2, NZ), 1 - half)
        z_copies[k] = (
            remote(ref_p, ref_p, zp_send.at[k], zp_recv.at[k], g, up),
            remote(ref_m, ref_m, zm_send.at[k], zm_recv.at[k], g, down),
        )
        for copy in z_copies[k]:
            copy.start()

    for copy in y_copies + packets:
        copy.start()
    for t in range(steps):
        x_step(t)
        if t >= 2 and t % 2 == 0 and (t - 2) // 2 < z_moves:
            z_step((t - 2) // 2)
    arrived(z_moves - 2)
    arrived(z_moves - 1)
    for copy in sib_copies + packets:
        copy.wait_recv()
    for t in range(steps - LAG, steps):
        for copy in x_copies[t]:
            copy.wait_recv()

    taking = jnp.logical_and(take[0] == 1, donor[0] != g)
    parent = jnp.where(taking, donor[0], g)
    k3 = kvec[...]
    parent_pos = pk_pos[parent]
    parent_small = pk_small[parent]

    def lane_of(packet, i):
        return packet[:, i : i + 1]

    hot_own = one_hot(lane_of(small, 0), ne)
    hot_parent = one_hot(lane_of(parent_small, 0), ne)
    hot_next = one_hot(column(moves[1]), ne)
    old_own = [pick(hot_own, pos[0, a : a + 1]) for a in range(3)]
    new_own = [old_own[a] + lane_of(small, 1 + a) for a in range(3)]
    old_par = [pick(hot_parent, parent_pos[a : a + 1]) for a in range(3)]
    new_par = [old_par[a] + lane_of(parent_small, 1 + a) for a in range(3)]
    was_moved = jnp.sum(hot_parent, 0, keepdims=True) > 0.0
    old_next, new_next = [], []
    for a in range(3):
        placed = jnp.sum(hot_parent * new_par[a], 0, keepdims=True)
        placed = jnp.where(was_moved, placed, parent_pos[a : a + 1])
        old_next.append(pick(hot_next, placed))
        new_next.append(old_next[a] + column(disp[1, 0, a : a + 1]))

    waves[0:16] = wave_rows(old_own, k3, False)
    waves[16:96] = wave_rows(new_own, k3, True)
    waves[96:112] = wave_rows(old_par, k3, False)
    waves[112:128] = wave_rows(new_par, k3, False)
    waves[128:144] = wave_rows(old_next, k3, False)
    waves[144:224] = wave_rows(new_next, k3, True)

    tile = min(256, ne)
    per = tile // K // 2

    @pl.loop(0, ne // tile)
    def _(i):
        block = cbuf[pl.ds(i * per, per)].reshape(tile, cbuf.shape[3])
        values[:, pl.ds(pl.multiple_of(i * tile, tile), tile)] = nt(waves[...], block)

    ahead_p = jnp.maximum(lax.rem(g - donor[0] + NX, NX), 1)
    ahead_m = jnp.maximum(lax.rem(donor[0] - g + NX, NX), 1)

    @pl.loop(0, chunks)
    def _(c):
        for half, got, ahead in ((0, rxp, ahead_p), (1, rxm, ahead_m)):
            rows = pl.ds(pl.multiple_of(half * (ne // 2) + c * CHUNK, CHUNK), CHUNK)
            hi, lo = split(mf[rows])
            mhi[rows] = jnp.where(taking, got[c + (ahead - 1) * LAG], hi)
            mlo[rows] = jnp.where(taking, jnp.zeros_like(lo), lo)

    hots = jnp.concatenate(
        [hot_own, hot_parent, hot_next, jnp.zeros((128 - 3 * K, ne), F32)], 0
    ).astype(BF16)

    @pl.loop(0, ne // tile)
    def _(i):
        rows = pl.ds(pl.multiple_of(i * tile, tile), tile)
        hi, lo = split(mf[rows])
        gath[0, rows] = nt(hi, hots) + nt(lo, hots)
        gath[1, rows] = nt(mhi[rows], hots) + nt(mlo[rows], hots)

    change_par = values[112:128] - values[96:112]
    change_next = values[144:160] - values[128:144]
    left_side = jnp.concatenate([change_par, change_next, values[160:224]], 0)
    left_hi, left_lo = split(left_side)
    left_both = jnp.concatenate([left_hi, left_lo], 0)
    count = left_side.shape[0]

    @pl.loop(0, ne // tile)
    def _(i):
        lanes = pl.ds(pl.multiple_of(i * tile, tile), tile)
        both = nn(left_both, mhi[:, lanes])
        amat[:, lanes] = both[:count] + both[count:] + nn(left_hi, mlo[:, lanes])

    wide_zero = jnp.zeros((128 - K, ne), F32)
    wide_parent = jnp.concatenate([hot_parent, wide_zero], 0)
    wide_next = jnp.concatenate([hot_next, wide_zero], 0)
    own_left = jnp.concatenate([values[16:32] - values[0:16], values[32:96]], 0)
    inside = iota((1, 128), 1) < K
    q_own = jnp.where(inside, nn(own_left, gath[0], HIGH), 0.0)
    q_par = nt(amat[...], wide_parent, HIGH)
    inverses, logs = invert(jnp.stack([augmented(q_own[:K]), augmented(q_par[:K])]))
    first = diagonals(nn(q_own[:, :K], inverses[0], HIGH))
    s0 = nn(inverses[1], amat[0:K], HIGH)
    b1 = amat[K:] - nn(q_par[K:, :K], s0, HIGH)
    q_next = nt(b1, wide_next, HIGH)
    inverse_next, log_next = invert(augmented(q_next[:K])[None])
    second = diagonals(nn(q_next[:, :K], inverse_next[0], HIGH))
    s1 = nn(inverse_next[0], b1[:K], HIGH)
    overlap = nt(s0, wide_next, HIGH)[:, :K]
    c0 = gath[1, :, K : 2 * K]
    c1 = gath[1, :, 2 * K : 3 * K] - nn(c0, overlap, HIGH)
    c0_hi, c0_lo = split(c0)
    c1_hi, c1_lo = split(c1)
    zeros = jnp.zeros((ne, 2 * K), BF16)
    ccat[...] = jnp.concatenate([c0_hi, c1_hi, c0_lo, c1_lo, c0_hi, c1_hi, zeros], 1)
    s0_hi, s0_lo = split(s0)
    s1_hi, s1_lo = split(s1)
    zeros = jnp.zeros((2 * K, ne), BF16)
    scat[...] = jnp.concatenate([s0_hi, s1_hi, s0_hi, s1_hi, s0_lo, s1_lo, zeros], 0)

    for update, rows in enumerate((first, second)):
        for a in range(3):
            drift[update, 0, a : a + 1] = rows[a]
        lap[update] = rows[3]
    weight[...] = parent_small[0:1, 4:5] + logs[1] + log_next[0]

    for t in range(steps):
        for copy in x_copies[t]:
            copy.wait_send()
    for copy in y_copies + packets + sib_copies:
        copy.wait_send()
    for k in range(z_moves):
        for copy in z_copies[k]:
            copy.wait_send()


def finish_kernel(mhi, mlo, ccat, scat, out):
    change = nn(ccat[...], scat[...])
    out[0] = (mhi[...].astype(F32) + mlo[...].astype(F32)) - change


def per_device(
    wavevectors, coefficients, inverse, positions, displacements, moved, donor, take, log_weight
):
    ne = inverse.shape[1]
    npw = coefficients.shape[0]
    steps = ne // 2 // CHUNK + 2 * LAG
    vmem = pl.BlockSpec(memory_space=pltpu.VMEM)
    smem = pl.BlockSpec(memory_space=pltpu.SMEM)
    dma = pltpu.SemaphoreType.DMA
    shape = jax.ShapeDtypeStruct
    mhi, mlo, ccat, scat, drift, lap, weight = pl.pallas_call(
        main_kernel,
        out_shape=(
            shape((ne, ne), BF16),
            shape((ne, ne), BF16),
            shape((ne, 128), BF16),
            shape((128, ne), BF16),
            shape((2, 1, 3, K), F32),
            shape((2, 1, K), F32),
            shape((1, 1), F32),
        ),
        in_specs=[smem, smem, smem, vmem, vmem, vmem, vmem, vmem, pl.BlockSpec(memory_space=pl.ANY)],
        out_specs=(vmem,) * 7,
        scratch_shapes=[
            pltpu.VMEM((ne, ne), F32),
            pltpu.VMEM((NZ * NY, 2, K, npw), BF16),
            pltpu.VMEM((ne // 2 // CHUNK, CHUNK, ne), BF16),
            pltpu.VMEM((ne // 2 // CHUNK, CHUNK, ne), BF16),
            pltpu.VMEM((steps, CHUNK, ne), BF16),
            pltpu.VMEM((steps, CHUNK, ne), BF16),
            pltpu.VMEM((NX, 3, ne), F32),
            pltpu.VMEM((NX, K, 128), F32),
            pltpu.VMEM((14 * K, npw), BF16),
            pltpu.VMEM((14 * K, ne), F32),
            pltpu.VMEM((2, ne, 128), F32),
            pltpu.VMEM((6 * K, ne), F32),
            dma(()), dma(()),
            dma((NY - 1,)), dma((NY - 1,)),
            dma((NX - 1,)), dma((NX - 1,)), dma((NX - 1,)), dma((NX - 1,)),
            dma((steps,)), dma((steps,)), dma((steps,)), dma((steps,)),
            dma((NZ - 1,)), dma((NZ - 1,)), dma((NZ - 1,)), dma((NZ - 1,)),
            dma((2,)), dma((2,)),
            dma((NZ - 1,)), dma((NZ - 1,)), dma((NZ - 1,)), dma((NZ - 1,)),
        ],
        compiler_params=pltpu.CompilerParams(
            collective_id=0, has_side_effects=True, vmem_limit_bytes=40 << 20
        ),
        name="exchange_and_update",
    )(
        donor, take, log_weight, wavevectors, positions, displacements, moved,
        coefficients.T, inverse,
    )
    rows = 128
    result = pl.pallas_call(
        finish_kernel,
        grid=(ne // rows,),
        out_shape=shape((1, ne, ne), F32),
        in_specs=[
            pl.BlockSpec((rows, ne), lambda i: (i, 0)),
            pl.BlockSpec((rows, ne), lambda i: (i, 0)),
            pl.BlockSpec((rows, 128), lambda i: (i, 0)),
            pl.BlockSpec((128, ne), lambda i: (0, 0)),
        ],
        out_specs=pl.BlockSpec((1, rows, ne), lambda i: (0, i, 0)),
        compiler_params=pltpu.CompilerParams(vmem_limit_bytes=16 << 20),
        name="rank_update",
    )(mhi, mlo, ccat, scat)
    return (result, drift, lap, weight.reshape(1))


def solution(mesh):
    return jax.shard_map(
        per_device,
        mesh=mesh,
        in_specs=(
            P(),
            P(None, "orb"),
            P(("grp", "orb"), None, None),
            P(("grp", "orb"), None, None),
            P(None, ("grp", "orb"), None, None),
            P(None, ("grp", "orb"), None),
            P("orb"),
            P(("grp", "orb")),
            P(("grp", "orb")),
        ),
        out_specs=(
            P(("grp", "orb"), None, None),
            P(None, ("grp", "orb"), None, None),
            P(None, ("grp", "orb"), None),
            P(("grp", "orb")),
        ),
        check_vma=False,
    )
```

```python
import jax
import jax.numpy as jnp
from jax import lax
from jax.experimental import pallas as pl
from jax.experimental.pallas import tpu as pltpu
from jax.sharding import PartitionSpec as P

F32 = jnp.float32
BF16 = jnp.bfloat16
NX, NY, NZ = 4, 4, 8
LAG = 5
CHUNK = 16
K = 16
HIGH = lax.Precision.HIGHEST
MESH = pl.DeviceIdType.MESH


def nn(a, b, precision=None):
    return lax.dot_general(
        a, b, (((1,), (0,)), ((), ())), precision=precision, preferred_element_type=F32
    )


def nt(a, b):
    return lax.dot_general(a, b, (((1,), (1,)), ((), ())), preferred_element_type=F32)


def split(a):
    hi = a.astype(BF16)
    return hi, (a - hi.astype(F32)).astype(BF16)


def iota(shape, dim):
    return lax.broadcasted_iota(jnp.int32, shape, dim)


def column(row):
    return jnp.sum(jnp.where(iota((K, K), 0) == iota((K, K), 1), row, 0.0), 1, keepdims=True)


def one_hot(indices, width):
    return jnp.where(iota((K, width), 1) == indices.astype(jnp.int32), 1.0, 0.0)


def pick(hot, row):
    return jnp.sum(hot * row, 1, keepdims=True)


def eliminate(state, k):
    a, pivots = state
    n = a.shape[0]
    row = iota((n, 1), 0)
    col = a[:, k : k + 1]
    size = jnp.where(row >= k, jnp.abs(col), -1.0)
    best = jnp.max(size, 0, keepdims=True)
    where = jnp.min(jnp.where(size == best, row, n), 0, keepdims=True)
    chosen = row == where
    pivot_row = jnp.sum(jnp.where(chosen, a, 0.0), 0, keepdims=True)
    pivot = pivot_row[:, k : k + 1]
    other = jnp.where(chosen, a[k : k + 1], a)
    factor = jnp.where(chosen, col[k : k + 1], col)
    scaled = pivot_row / pivot
    a = jnp.where(row == k, scaled, other - factor * scaled)
    pivots = jnp.where(iota(pivots.shape, 1) == k, pivot, pivots)
    return a, pivots


def augmented(x):
    n = x.shape[0]
    r, c = iota(x.shape, 0), iota(x.shape, 1)
    return jnp.where(c < n, x, 0.0) + jnp.where((c == r) | (c == r + n), 1.0, 0.0)


def wave_rows(points, kvec):
    phases = points[0] * kvec[0:1] + points[1] * kvec[1:2]
    phases = phases + points[2] * kvec[2:3]
    return jnp.cos(phases).astype(BF16), jnp.sin(phases).astype(BF16)


def slope_rows(waves, kvec):
    cos, sin = waves[0].astype(F32), waves[1].astype(F32)
    rows = []
    for a in range(3):
        k = kvec[a : a + 1]
        rows.append(((-k * sin).astype(BF16), (k * cos).astype(BF16)))
    square = kvec[0:1] * kvec[0:1] + kvec[1:2] * kvec[1:2] + kvec[2:3] * kvec[2:3]
    rows.append(((-square * cos).astype(BF16), (-square * sin).astype(BF16)))
    return rows


def diagonals(block):
    eye = iota((K, K), 0) == iota((K, K), 1)
    return [
        jnp.sum(jnp.where(eye, block[K * i : K * (i + 1)], 0.0), 0, keepdims=True)
        for i in range(4)
    ]


def main_kernel(
    donor, take, log_weight, kvec_in, pos_in, disp_in, moved_in, coef, inverse,
    mhi, mlo, ccat, scat, drift, lap, weight,
    mf, cbuf, sx, rx, kvec, pk_pos, pk_disp, pk_moved, pk_log, waves, values, cown,
    m_sem, c_sem, y_send, y_recv, p_send, p_recv, x_send, x_recv,
    z_send, z_recv, s_send, s_recv,
):
    ne, ng = mf.shape[0], kvec.shape[1]
    steps = rx.shape[1]
    total = ne // CHUNK
    g = lax.axis_index("grp")
    o = lax.axis_index("orb")
    core, y, z = lax.rem(o, 2), lax.rem(o // 2, NY), o // (2 * NY)

    def orb(zz, yy, cc):
        return (zz * NY + yy) * 2 + cc

    def turn(value, by, size):
        return lax.rem(value + by + size, size)

    def remote(src, dst, send, recv, grp, orb_index):
        return pltpu.make_async_remote_copy(
            src_ref=src, dst_ref=dst, send_sem=send, recv_sem=recv,
            device_id=(grp, orb_index), device_id_type=MESH,
        )

    def shard(zz, yy, cc=core):
        return cbuf.at[zz * NY + yy, cc]

    pieces = m_sem.shape[0]
    piece = ne // pieces
    loads = []
    for i in range(pieces):
        rows = pl.ds(i * piece, piece)
        loads.append(pltpu.make_async_copy(inverse.at[0, rows], mf.at[rows], m_sem.at[i]))
    for i in range(pieces // 2):
        loads[i].start()
        loads[pieces - 1 - i].start()
    small = [
        pltpu.make_async_copy(src, dst, c_sem.at[i])
        for i, (src, dst) in enumerate(
            (
                (kvec_in, kvec),
                (pos_in, pk_pos.at[g]),
                (disp_in, pk_disp.at[g]),
                (moved_in, pk_moved.at[g]),
                (coef, shard(z, y)),
            )
        )
    ]
    for copy in small:
        copy.start()
    pk_log[g] = jnp.full((8, 128), log_weight[0], F32)

    barrier = pltpu.get_barrier_semaphore()
    up, down = orb(turn(z, 1, NZ), y, core), orb(turn(z, -1, NZ), y, core)
    sibling = orb(z, y, 1 - core)
    partners = [(turn(g, d, NX), o) for d in range(1, NX)]
    partners += [(g, orb(z, turn(y, d, NY), core)) for d in range(1, NY)]
    partners += [(g, up), (g, down), (g, sibling)]
    for partner in partners:
        pl.semaphore_signal(barrier, inc=1, device_id=partner, device_id_type=MESH)
    pl.semaphore_wait(barrier, len(partners))

    is_source = donor[0] == g
    right, left = turn(g, 1, NX), turn(g, -1, NX)
    x_copies = {}

    def x_arrived(t):
        for copy in x_copies[t]:
            copy.wait_recv()

    def x_step(t):
        if t >= LAG:
            x_arrived(t - LAG)
        for way, first in ((0, t * CHUNK), (1, ne - (t + 1) * CHUNK)):
            own = mf[first : first + CHUNK].astype(BF16)
            sx[way, t] = jnp.where(is_source, own, rx[way, t - LAG]) if t >= LAG else own
        x_copies[t] = [
            remote(sx.at[way, t], rx.at[way, t], x_send.at[way, t], x_recv.at[way, t], to, o)
            for way, to in ((0, right), (1, left))
        ]
        for copy in x_copies[t]:
            copy.start()

    taking = jnp.logical_and(take[0] == 1, donor[0] != g)
    ahead = lax.rem(g - donor[0] + NX, NX)

    def places_of(r):
        found = []
        for hops in range(1, NX):
            t = r + (hops - 1) * LAG
            if t < steps:
                found.append((0, t))
            else:
                found.append((1, total - 1 - r + (NX - hops - 1) * LAG))
        return found

    ready = {}
    for r in range(total):
        ready.setdefault(max(t for _, t in places_of(r)), []).append(r)

    def select(r):
        rows = pl.ds(r * CHUNK, CHUNK)
        hi, lo = split(mf[rows])
        one, two, three = (rx[way, t] for way, t in places_of(r))
        got = jnp.where(ahead == 1, one, jnp.where(ahead == 2, two, three))
        mhi[rows] = jnp.where(taking, got, hi)
        mlo[rows] = jnp.where(taking, jnp.zeros_like(lo), lo)

    y_copies = [
        remote(coef, shard(z, y), y_send.at[d - 1], y_recv.at[d - 1], g,
               orb(z, turn(y, d, NY), core))
        for d in range(1, NY)
    ]
    laps = NY * (NZ - 1) // 2
    full = NY * (NZ // 2 - 1)
    rest = laps - full
    z_copies, s_copies, seen = {}, {}, set()

    def item(way, k):
        if k < full:
            return k // NY, k % NY
        return NZ // 2 - 1, k - full + (rest if way else 0)

    def place(way, m, j):
        return shard(turn(z, m if way else -m, NZ), turn(y, j, NY))

    def to_sibling(index, src, dst):
        s_copies[index] = remote(src, dst, s_send.at[index], s_recv.at[index], g, sibling)
        s_copies[index].start()

    def z_arrived(way, k):
        if (way, k) not in seen:
            seen.add((way, k))
            z_copies[way, k].wait_recv()
            m, j = item(way, k)
            got = place(way, m + 1, j)
            to_sibling(NY + way * laps + k, got, got)

    def z_step(k):
        if k < laps:
            for way in range(2):
                m, j = item(way, k)
                src = dst = place(way, m, j)
                if m:
                    z_arrived(way, k - NY if k < full else full - NY + j)
                elif j == 0:
                    src = coef
                elif way == 0:
                    y_copies[NY - j - 1].wait_recv()
                z_copies[way, k] = remote(
                    src, dst, z_send.at[way, k], z_recv.at[way, k], g, (up, down)[way]
                )
                z_copies[way, k].start()
                if m == 0 and way == 0:
                    to_sibling(j, src, dst)
        if k >= NY:
            for way in range(2):
                z_arrived(way, k - NY)

    packets = []
    for d in range(1, NX):
        for i, (src, all_slots) in enumerate(
            ((pos_in, pk_pos), (disp_in, pk_disp), (moved_in, pk_moved), (pk_log.at[g], pk_log))
        ):
            packets.append(
                remote(src, all_slots.at[g], p_send.at[d - 1, i], p_recv.at[d - 1, i],
                       turn(g, d, NX), o)
            )
    known = {}

    def find_points():
        for copy in packets:
            copy.wait_recv()
        for copy in small:
            copy.wait()
        parent = jnp.where(taking, donor[0], g)
        hot_own = one_hot(column(pk_moved[g, 0].astype(F32)), ne)
        hot_par = one_hot(column(pk_moved[parent, 0].astype(F32)), ne)
        hot_next = one_hot(column(pk_moved[g, 1].astype(F32)), ne)
        old_own = [pick(hot_own, pk_pos[g, a]) for a in range(3)]
        new_own = [old_own[a] + column(pk_disp[g, a]) for a in range(3)]
        old_par = [pick(hot_par, pk_pos[parent, a]) for a in range(3)]
        new_par = [old_par[a] + column(pk_disp[parent, a]) for a in range(3)]
        was_moved = jnp.sum(hot_par, 0, keepdims=True) > 0.0
        old_next = []
        for a in range(3):
            placed = jnp.sum(hot_par * new_par[a], 0, keepdims=True)
            old_next.append(pick(hot_next, jnp.where(was_moved, placed, pk_pos[parent, a])))
        new_next = [old_next[a] + column(pk_disp[g, 3 + a]) for a in range(3)]
        known["points"] = (old_own, old_par, new_par, old_next, new_own, new_next)
        zeros = jnp.zeros((2 * K, ne), F32)
        pair = jnp.concatenate([hot_par, hot_next], 0)
        known["hi"] = jnp.concatenate([pair, zeros, pair, zeros], 0).astype(BF16)
        known["lo"] = jnp.concatenate([zeros, pair, zeros, zeros], 0).astype(BF16)
        wide = jnp.zeros((128 - 2 * K, ne), F32)
        none = jnp.zeros((K, ne), F32)
        known["own_hi"] = jnp.concatenate([hot_own, none, wide], 0).astype(BF16)
        known["own_lo"] = jnp.concatenate([none, hot_own, wide], 0).astype(BF16)
        known["log"] = pk_log[parent]

    def find_waves(i):
        pair = wave_rows(known["points"][i], kvec[...])
        first = i * K if i < 4 else 4 * K + (i - 4) * 5 * K
        rows = [pair] + (slope_rows(pair, kvec[...]) if i >= 4 else [])
        for n, (cos, sin) in enumerate(rows):
            waves[first + n * K : first + (n + 1) * K, :ng] = cos
            waves[first + n * K : first + (n + 1) * K, ng:] = sin

    block = 2 * NY * K

    def find_values(m):
        ends = [turn(z, m, NZ), turn(z, -m, NZ)] if m else [z, turn(z, NZ // 2, NZ)]
        table = jnp.concatenate(
            [cbuf[pl.ds(e * NY, NY)].reshape(block, cbuf.shape[3]) for e in ends], 0
        )
        result = nt(waves[...], table)
        for i, e in enumerate(ends):
            lanes = pl.ds(pl.multiple_of(e * block, block), block)
            values[:, lanes] = result[:, i * block : (i + 1) * block]

    def s_wait(m):
        count = 0
        for way in range(2):
            for k in range(laps):
                if item(way, k)[0] + 1 == m:
                    s_copies[NY + way * laps + k].wait_recv()
                    count += 1

    tile = min(256, ne)

    def own_columns(i):
        rows = pl.ds(i * tile, tile)
        hi, lo = split(mf[rows])
        cown[rows] = (nt(hi, known["own_hi"]) + nt(lo, known["own_lo"])).astype(BF16)

    def columns(i):
        rows = pl.ds(i * tile, tile)
        ccat[rows] = (nt(mhi[rows], known["hi"]) + nt(mlo[rows], known["lo"])).astype(BF16)

    tiles = ne // tile
    work = {}

    def plan(t, what, *args):
        work.setdefault(min(t, steps - 1), []).append((what, args))

    plan(7, find_points)
    for i in range(6):
        plan(8 + i, find_waves, i)
    for i in range(tiles):
        plan(15 + i, own_columns, i)
    for m in range(1, NZ // 2 - 1):
        plan(14 + 6 * m, lambda m: (s_wait(m), find_values(m)), m)

    for t in range(steps):
        for i in range(pieces // 2):
            if t == 2 * i:
                loads[i].wait()
                loads[pieces - 1 - i].wait()
        x_step(t)
        if t == 0:
            for copy in y_copies + packets:
                copy.start()
        if t >= LAG:
            for r in ready.get(t - LAG, ()):
                select(r)
        if t % 2 == 0 and t // 2 < laps + NY:
            z_step(t // 2)
        for what, args in work.get(t, ()):
            what(*args)
    for k in range((steps + 1) // 2, laps + NY):
        z_step(k)
    for m in range(NY):
        s_copies[m].wait_recv()
    s_wait(NZ // 2 - 1)
    find_values(NZ // 2 - 1)
    for t in range(steps - LAG, steps):
        x_arrived(t)
        for r in ready.get(t, ()):
            select(r)
    for i in range(tiles):
        columns(i)
    s_wait(NZ // 2)
    find_values(0)

    def stacked(rows):
        hi, lo = split(rows)
        return jnp.concatenate([hi, lo], 0)

    base, second = 4 * K, 9 * K
    own_left = stacked(
        jnp.concatenate([values[base : base + K] - values[0:K], values[base + K : second]], 0)
    )
    changes = jnp.concatenate(
        [values[2 * K : 3 * K] - values[K : 2 * K], values[second : second + K] - values[3 * K : base]], 0
    )
    slopes = values[second + K :]
    left = stacked(jnp.concatenate([changes, slopes], 0))
    cut = own_left.shape[0] // 2
    own_got = nn(own_left, cown[...])
    own_g = own_got[:cut] + own_got[cut:]
    own_g = own_g[:, :K] + own_got[:cut, K : 2 * K]
    cut = left.shape[0] // 2
    got = nn(left, ccat[...])
    lanes = got[:cut] + got[cut:]
    ratio_g = lanes[:, : 2 * K] + got[:cut, 2 * K : 4 * K]

    def widen(x):
        return jnp.concatenate([x, jnp.zeros((x.shape[0], 128 - x.shape[1]), F32)], 1)

    ones = jnp.ones((1, 128), F32)
    state = (augmented(widen(ratio_g[: 2 * K])), ones)
    own_state = (augmented(widen(own_g[:K])), ones)
    for k in range(2 * K):
        state = eliminate(state, k)
        if k < K:
            own_state = eliminate(own_state, k)
    own_inverse = own_state[0][:, K : 2 * K]
    inverse_32 = state[0][:, 2 * K : 4 * K]
    change_hi, change_lo = split(changes)
    change_both = jnp.concatenate([change_hi, change_lo], 0)
    product = nn(change_both, mhi[...])
    product = product[: 2 * K] + product[2 * K :] + nn(change_hi, mlo[...])
    solved = nn(inverse_32, product, HIGH)
    solved_hi, solved_lo = split(solved)
    scat[...] = jnp.concatenate(
        [solved_hi, solved_hi, solved_lo, jnp.zeros((2 * K, ne), BF16)], 0
    )
    first_rows = diagonals(nn(own_g[K:], own_inverse, HIGH))
    next_rows = diagonals(nn(ratio_g[2 * K :], inverse_32[:, K:], HIGH))
    for update, rows in enumerate((first_rows, next_rows)):
        for a in range(3):
            drift[3 * update + a] = rows[a]
        lap[update] = rows[3]
    logs = jnp.sum(jnp.log(jnp.abs(state[1])), 1, keepdims=True)
    weight[...] = known["log"][0:1, 0:1] + logs

    for copy in y_copies + packets + list(z_copies.values()) + list(s_copies.values()):
        copy.wait_send()
    for copies in x_copies.values():
        for copy in copies:
            copy.wait_send()


def finish_kernel(mhi, mlo, ccat, scat, drift_in, lap_in, weight_in,
                  out, drift, lap, weight, rows_f, sems):
    parts = sems.shape[0]
    size = mhi.shape[0] // parts
    copies = []
    for i in range(parts):
        rows = pl.ds(i * size, size)
        change = nn(ccat[rows], scat[...])
        rows_f[rows] = (mhi[rows].astype(F32) + mlo[rows].astype(F32)) - change
        copies.append(pltpu.make_async_copy(rows_f.at[rows], out.at[0, rows], sems.at[i]))
        copies[-1].start()
    drift[...] = drift_in[...]
    lap[...] = lap_in[...]
    weight[...] = weight_in[...]
    for copy in copies:
        copy.wait()


def per_device(
    wavevectors, coefficients, inverse, positions, displacements, moved, donor, take, log_weight
):
    ne = inverse.shape[1]
    npw = coefficients.shape[0]
    ng = wavevectors.shape[1]
    steps = ne // 2 // CHUNK + LAG
    laps = NY * (NZ - 1) // 2
    vmem = pl.BlockSpec(memory_space=pltpu.VMEM)
    smem = pl.BlockSpec(memory_space=pltpu.SMEM)
    hbm = pl.BlockSpec(memory_space=pltpu.HBM)
    dma = pltpu.SemaphoreType.DMA
    shape = jax.ShapeDtypeStruct
    smalls = (shape((6, 1, K), F32), shape((2, 1, K), F32), shape((1, 1), F32))
    states = pl.pallas_call(
        main_kernel,
        out_shape=(
            shape((ne, ne), BF16),
            shape((ne, ne), BF16),
            shape((ne, 128), BF16),
            shape((128, ne), BF16),
        )
        + smalls,
        in_specs=[smem] * 3 + [hbm] * 6,
        out_specs=(vmem,) * 7,
        scratch_shapes=[
            pltpu.VMEM((ne, ne), F32),
            pltpu.VMEM((NZ * NY, 2, K, npw), BF16),
            pltpu.VMEM((2, steps, CHUNK, ne), BF16),
            pltpu.VMEM((2, steps, CHUNK, ne), BF16),
            pltpu.VMEM((3, ng), F32),
            pltpu.VMEM((NX, 3, 1, ne), F32),
            pltpu.VMEM((NX, 6, 1, K), F32),
            pltpu.VMEM((NX, 2, 1, K), jnp.int32),
            pltpu.VMEM((NX, 8, 128), F32),
            pltpu.VMEM((14 * K, npw), BF16),
            pltpu.VMEM((14 * K, ne), F32),
            pltpu.VMEM((ne, 128), BF16),
            dma((8,)),
            dma((5,)),
            dma((NY - 1,)),
            dma((NY - 1,)),
            dma((NX - 1, 4)),
            dma((NX - 1, 4)),
            dma((2, steps)),
            dma((2, steps)),
            dma((2, laps)),
            dma((2, laps)),
            dma((NY + 2 * laps,)),
            dma((NY + 2 * laps,)),
        ],
        compiler_params=pltpu.CompilerParams(
            collective_id=0, has_side_effects=True, vmem_limit_bytes=40 << 20
        ),
        name="exchange_and_update",
    )(
        donor,
        take,
        log_weight,
        *(
            pltpu.with_memory_space_constraint(x, pltpu.HBM)
            for x in (
                wavevectors,
                positions.transpose(1, 0, 2),
                displacements.reshape(6, 1, K),
                moved,
                coefficients.T,
                inverse,
            )
        ),
    )
    result, drift, lap, weight = pl.pallas_call(
        finish_kernel,
        out_shape=(shape((1, ne, ne), F32),) + smalls,
        in_specs=[vmem] * 7,
        out_specs=(hbm,) + (vmem,) * 3,
        scratch_shapes=[pltpu.VMEM((ne, ne), F32), dma((8,))],
        compiler_params=pltpu.CompilerParams(vmem_limit_bytes=16 << 20),
        name="rank_update",
    )(*states)
    return (result, drift.reshape(2, 1, 3, K), lap, weight.reshape(1))


def solution(mesh):
    return jax.shard_map(
        per_device,
        mesh=mesh,
        in_specs=(
            P(),
            P(None, "orb"),
            P(("grp", "orb"), None, None),
            P(("grp", "orb"), None, None),
            P(None, ("grp", "orb"), None, None),
            P(None, ("grp", "orb"), None),
            P("orb"),
            P(("grp", "orb")),
            P(("grp", "orb")),
        ),
        out_specs=(
            P(("grp", "orb"), None, None),
            P(None, ("grp", "orb"), None, None),
            P(None, ("grp", "orb"), None),
            P(("grp", "orb")),
        ),
        check_vma=False,
    )
```

```python
import jax
import jax.numpy as jnp
from jax import lax
from jax.experimental import pallas as pl
from jax.experimental.pallas import tpu as pltpu
from jax.sharding import PartitionSpec as P

F32 = jnp.float32
BF16 = jnp.bfloat16
NX, NY, NZ = 4, 4, 8
LAG = 6
VALUE_STEPS = (19, 26, 34)
CHUNK = 16
K = 16
HIGH = lax.Precision.HIGHEST
MESH = pl.DeviceIdType.MESH


def nn(a, b, precision=None):
    return lax.dot_general(
        a, b, (((1,), (0,)), ((), ())), precision=precision, preferred_element_type=F32
    )


def nt(a, b):
    return lax.dot_general(a, b, (((1,), (1,)), ((), ())), preferred_element_type=F32)


def split(a):
    hi = a.astype(BF16)
    return hi, (a - hi.astype(F32)).astype(BF16)


def iota(shape, dim):
    return lax.broadcasted_iota(jnp.int32, shape, dim)


def column(row):
    return jnp.sum(jnp.where(iota((K, K), 0) == iota((K, K), 1), row, 0.0), 1, keepdims=True)


def one_hot(indices, width):
    return jnp.where(iota((K, width), 1) == indices.astype(jnp.int32), 1.0, 0.0)


def pick(hot, row):
    return jnp.sum(hot * row, 1, keepdims=True)


def eliminate(state, k):
    a, pivots = state
    row = iota(a.shape, 0)
    col = jnp.broadcast_to(a[:, k : k + 1], a.shape)
    size = jnp.abs(col)
    scaled = size * 257.0
    key = (scaled - (scaled - size)) * (1.0 + row.astype(F32) * 2.0**-22)
    key = jnp.where(row >= k, key, -1.0)
    chosen = key == jnp.max(key, 0, keepdims=True)
    pivot_row = jnp.sum(jnp.where(chosen, a, 0.0), 0, keepdims=True)
    pivot = jnp.sum(jnp.where(chosen, col, 0.0), 0, keepdims=True)
    other = jnp.where(chosen, a[k : k + 1], a)
    factor = jnp.where(chosen, col[k : k + 1], col)
    pivot_row = pivot_row * (1.0 / pivot)
    a = jnp.where(row == k, pivot_row, other - factor * pivot_row)
    pivots = jnp.where(iota(pivots.shape, 1) == k, pivot, pivots)
    return a, pivots


def augmented(x):
    n = x.shape[0]
    r, c = iota(x.shape, 0), iota(x.shape, 1)
    return jnp.where(c < n, x, 0.0) + jnp.where((c == r) | (c == r + n), 1.0, 0.0)


def wave_rows(points, kvec):
    phases = points[0] * kvec[0:1] + points[1] * kvec[1:2]
    phases = phases + points[2] * kvec[2:3]
    return jnp.cos(phases).astype(BF16), jnp.sin(phases).astype(BF16)


def slope_rows(waves, kvec):
    cos, sin = waves[0].astype(F32), waves[1].astype(F32)
    rows = []
    for a in range(3):
        k = kvec[a : a + 1]
        rows.append(((-k * sin).astype(BF16), (k * cos).astype(BF16)))
    square = kvec[0:1] * kvec[0:1] + kvec[1:2] * kvec[1:2] + kvec[2:3] * kvec[2:3]
    rows.append(((-square * cos).astype(BF16), (-square * sin).astype(BF16)))
    return rows


def diagonals(block):
    eye = iota((K, K), 0) == iota((K, K), 1)
    return [
        jnp.sum(jnp.where(eye, block[K * i : K * (i + 1)], 0.0), 0, keepdims=True)
        for i in range(4)
    ]


def main_kernel(
    donor, take, log_weight, kvec_in, pos_in, disp_in, moved_in, coef, inverse,
    chosen, ccat, scat, drift, lap, weight,
    mf, mhi, mlo, cbuf, sx, rx, kvec, pk_pos, pk_disp, pk_moved, pk_log, waves, values, cown,
    m_sem, c_sem, y_send, y_recv, p_send, p_recv, x_send, x_recv,
    z_send, z_recv, s_send, s_recv,
):
    ne, ng = mf.shape[0], kvec.shape[1]
    steps = rx.shape[1]
    total = ne // CHUNK
    g = lax.axis_index("grp")
    o = lax.axis_index("orb")
    core, y, z = lax.rem(o, 2), lax.rem(o // 2, NY), o // (2 * NY)

    def orb(zz, yy, cc):
        return (zz * NY + yy) * 2 + cc

    def turn(value, by, size):
        return lax.rem(value + by + size, size)

    def remote(src, dst, send, recv, grp, orb_index):
        return pltpu.make_async_remote_copy(
            src_ref=src, dst_ref=dst, send_sem=send, recv_sem=recv,
            device_id=(grp, orb_index), device_id_type=MESH,
        )

    def shard(zz, yy, cc=core):
        return cbuf.at[zz * NY + yy, cc]

    barrier = pltpu.get_barrier_semaphore()
    up, down = orb(turn(z, 1, NZ), y, core), orb(turn(z, -1, NZ), y, core)
    sibling = orb(z, y, 1 - core)
    partners = [(turn(g, d, NX), o) for d in range(1, NX)]
    partners += [(g, orb(z, turn(y, d, NY), core)) for d in range(1, NY)]
    partners += [(g, up), (g, down), (g, sibling)]
    for partner in partners:
        pl.semaphore_signal(barrier, inc=1, device_id=partner, device_id_type=MESH)

    pieces = m_sem.shape[0]
    piece = ne // pieces
    loads = []
    for i in range(pieces):
        rows = pl.ds(i * piece, piece)
        loads.append(pltpu.make_async_copy(inverse.at[0, rows], mf.at[rows], m_sem.at[i]))
    for i in range(pieces // 2):
        loads[i].start()
        loads[pieces - 1 - i].start()
    small = [
        pltpu.make_async_copy(src, dst, c_sem.at[i])
        for i, (src, dst) in enumerate(
            (
                (kvec_in, kvec),
                (pos_in, pk_pos.at[g]),
                (disp_in, pk_disp.at[g]),
                (moved_in, pk_moved.at[g]),
                (coef, shard(z, y)),
            )
        )
    ]
    for copy in small:
        copy.start()
    pk_log[g] = jnp.full((8, 128), log_weight[0], F32)
    pl.semaphore_wait(barrier, len(partners))

    is_source = donor[0] == g
    right, left = turn(g, 1, NX), turn(g, -1, NX)
    x_copies = {}

    def x_arrived(t):
        for copy in x_copies[t]:
            copy.wait_recv()

    def x_step(t):
        if t >= LAG:
            x_arrived(t - LAG)
        for way, first in ((0, t * CHUNK), (1, ne - (t + 1) * CHUNK)):
            own = mf[first : first + CHUNK].astype(BF16)
            sx[way, t] = jnp.where(is_source, own, rx[way, t - LAG]) if t >= LAG else own
        x_copies[t] = [
            remote(sx.at[way, t], rx.at[way, t], x_send.at[way, t], x_recv.at[way, t], to, o)
            for way, to in ((0, right), (1, left))
        ]
        for copy in x_copies[t]:
            copy.start()

    taking = jnp.logical_and(take[0] == 1, donor[0] != g)
    ahead = lax.rem(g - donor[0] + NX, NX)

    def places_of(r):
        found = []
        for hops in range(1, NX):
            t = r + (hops - 1) * LAG
            if t < steps:
                found.append((0, t))
            else:
                found.append((1, total - 1 - r + (NX - hops - 1) * LAG))
        return found

    ready = {}
    for r in range(total):
        ready.setdefault(max(t for _, t in places_of(r)), []).append(r)

    def select(r):
        rows = pl.ds(r * CHUNK, CHUNK)
        hi, lo = split(mf[rows])
        one, two, three = (rx[way, t] for way, t in places_of(r))
        got = jnp.where(ahead == 1, one, jnp.where(ahead == 2, two, three))
        mhi[rows] = jnp.where(taking, got, hi)
        mlo[rows] = jnp.where(taking, jnp.zeros_like(lo), lo)
        chosen[rows] = jnp.where(taking, got.astype(F32), mf[rows])

    y_copies = [
        remote(coef, shard(z, y), y_send.at[d - 1], y_recv.at[d - 1], g,
               orb(z, turn(y, d, NY), core))
        for d in range(1, NY)
    ]
    laps = NY * (NZ - 1) // 2
    full = NY * (NZ // 2 - 1)
    rest = laps - full
    z_copies, s_copies, seen = {}, {}, set()

    def item(way, k):
        if k < full:
            return k // NY, k % NY
        return NZ // 2 - 1, k - full + (rest if way else 0)

    def place(way, m, j):
        return shard(turn(z, m if way else -m, NZ), turn(y, j, NY))

    def to_sibling(index, src, dst):
        s_copies[index] = remote(src, dst, s_send.at[index], s_recv.at[index], g, sibling)
        s_copies[index].start()

    def z_arrived(way, k):
        if (way, k) not in seen:
            seen.add((way, k))
            z_copies[way, k].wait_recv()
            m, j = item(way, k)
            got = place(way, m + 1, j)
            to_sibling(NY + way * laps + k, got, got)

    def z_step(k):
        if k < laps:
            for way in range(2):
                m, j = item(way, k)
                src = dst = place(way, m, j)
                if m:
                    z_arrived(way, k - NY if k < full else full - NY + j)
                elif j == 0:
                    src = coef
                elif way == 0:
                    y_copies[NY - j - 1].wait_recv()
                z_copies[way, k] = remote(
                    src, dst, z_send.at[way, k], z_recv.at[way, k], g, (up, down)[way]
                )
                z_copies[way, k].start()
                if m == 0 and way == 0:
                    to_sibling(j, src, dst)
        if k >= NY:
            for way in range(2):
                z_arrived(way, k - NY)

    packets = []
    for d in range(1, NX):
        for i, (src, all_slots) in enumerate(
            ((pos_in, pk_pos), (disp_in, pk_disp), (moved_in, pk_moved), (pk_log.at[g], pk_log))
        ):
            packets.append(
                remote(src, all_slots.at[g], p_send.at[d - 1, i], p_recv.at[d - 1, i],
                       turn(g, d, NX), o)
            )
    known = {}

    def find_points():
        for copy in packets:
            copy.wait_recv()
        for copy in small:
            copy.wait()
        parent = jnp.where(taking, donor[0], g)
        hot_own = one_hot(column(pk_moved[g, 0].astype(F32)), ne)
        hot_par = one_hot(column(pk_moved[parent, 0].astype(F32)), ne)
        hot_next = one_hot(column(pk_moved[g, 1].astype(F32)), ne)
        old_own = [pick(hot_own, pk_pos[g, a]) for a in range(3)]
        new_own = [old_own[a] + column(pk_disp[g, a]) for a in range(3)]
        old_par = [pick(hot_par, pk_pos[parent, a]) for a in range(3)]
        new_par = [old_par[a] + column(pk_disp[parent, a]) for a in range(3)]
        was_moved = jnp.sum(hot_par, 0, keepdims=True) > 0.0
        old_next = []
        for a in range(3):
            placed = jnp.sum(hot_par * new_par[a], 0, keepdims=True)
            old_next.append(pick(hot_next, jnp.where(was_moved, placed, pk_pos[parent, a])))
        new_next = [old_next[a] + column(pk_disp[g, 3 + a]) for a in range(3)]
        known["points"] = (old_own, old_par, new_par, old_next, new_own, new_next)
        zeros = jnp.zeros((2 * K, ne), F32)
        pair = jnp.concatenate([hot_par, hot_next], 0)
        known["hi"] = jnp.concatenate([pair, zeros, pair, zeros], 0).astype(BF16)
        known["lo"] = jnp.concatenate([zeros, pair, zeros, zeros], 0).astype(BF16)
        wide = jnp.zeros((128 - 2 * K, ne), F32)
        none = jnp.zeros((K, ne), F32)
        known["own_hi"] = jnp.concatenate([hot_own, none, wide], 0).astype(BF16)
        known["own_lo"] = jnp.concatenate([none, hot_own, wide], 0).astype(BF16)
        known["log"] = pk_log[parent]

    def find_waves(i):
        pair = wave_rows(known["points"][i], kvec[...])
        first = i * K if i < 4 else 4 * K + (i - 4) * 5 * K
        rows = [pair] + (slope_rows(pair, kvec[...]) if i >= 4 else [])
        for n, (cos, sin) in enumerate(rows):
            waves[first + n * K : first + (n + 1) * K, :ng] = cos
            waves[first + n * K : first + (n + 1) * K, ng:] = sin

    block = 2 * NY * K

    def find_values(m):
        ends = [turn(z, m + 1, NZ), turn(z, -m, NZ)]
        table = jnp.concatenate(
            [cbuf[pl.ds(e * NY, NY)].reshape(block, cbuf.shape[3]) for e in ends], 0
        )
        result = nt(waves[...], table)
        for i, e in enumerate(ends):
            lanes = pl.ds(pl.multiple_of(e * block, block), block)
            values[:, lanes] = result[:, i * block : (i + 1) * block]

    def s_wait(m):
        for way in range(2):
            for k in range(laps):
                offset = item(way, k)[0] + 1
                if offset == (m + 1 if way else m) or offset == m + 1 == NZ // 2:
                    s_copies[NY + way * laps + k].wait_recv()
        if m == 0:
            for j in range(NY):
                s_copies[j].wait_recv()

    tile = min(256, ne)

    def own_columns(i):
        rows = pl.ds(i * tile, tile)
        hi, lo = split(mf[rows])
        cown[rows] = (nt(hi, known["own_hi"]) + nt(lo, known["own_lo"])).astype(BF16)

    def columns(i):
        rows = pl.ds(i * tile, tile)
        ccat[rows] = (nt(mhi[rows], known["hi"]) + nt(mlo[rows], known["lo"])).astype(BF16)

    tiles = ne // tile
    work = {}

    def plan(t, what, *args):
        work.setdefault(min(t, steps - 1), []).append((what, args))

    plan(8, find_points)
    for i in range(6):
        plan(9 + i, find_waves, i)
    for i in range(tiles):
        plan(15 + i, own_columns, i)
    early = [i for i in (0, tiles - 1) if tiles > 2]
    for i in early:
        plan(steps - 3 + (i > 0), columns, i)
    for m in range(NZ // 2 - 1):
        plan(VALUE_STEPS[m], lambda m: (s_wait(m), find_values(m)), m)

    for t in range(steps):
        for i in range(pieces // 2):
            if t == 2 * i:
                loads[i].wait()
                loads[pieces - 1 - i].wait()
        x_step(t)
        if t == 0:
            for copy in y_copies + packets:
                copy.start()
        if t >= LAG:
            for r in ready.get(t - LAG, ()):
                select(r)
        if t % 2 == 0 and t // 2 < laps + NY:
            z_step(t // 2)
        for what, args in work.get(t, ()):
            what(*args)
    for k in range((steps + 1) // 2, laps + NY):
        z_step(k)
    for t in range(steps - LAG, steps):
        x_arrived(t)
        for r in ready.get(t, ()):
            select(r)
    for i in range(tiles):
        if i not in early:
            columns(i)
    s_wait(NZ // 2 - 1)
    find_values(NZ // 2 - 1)

    def stacked(rows):
        hi, lo = split(rows)
        return jnp.concatenate([hi, lo], 0)

    base, second = 4 * K, 9 * K
    own_left = stacked(
        jnp.concatenate([values[base : base + K] - values[0:K], values[base + K : second]], 0)
    )
    changes = jnp.concatenate(
        [values[2 * K : 3 * K] - values[K : 2 * K], values[second : second + K] - values[3 * K : base]], 0
    )
    slopes = values[second + K :]
    left = stacked(jnp.concatenate([changes, slopes], 0))
    cut = own_left.shape[0] // 2
    own_got = nn(own_left, cown[...])
    own_g = own_got[:cut] + own_got[cut:]
    own_g = own_g[:, :K] + own_got[:cut, K : 2 * K]
    cut = left.shape[0] // 2
    got = nn(left, ccat[...])
    lanes = got[:cut] + got[cut:]
    ratio_g = lanes[:, : 2 * K] + got[:cut, 2 * K : 4 * K]

    def widen(x):
        return jnp.concatenate([x, jnp.zeros((x.shape[0], 128 - x.shape[1]), F32)], 1)

    ones = jnp.ones((1, 128), F32)
    state = (augmented(widen(ratio_g[: 2 * K])), ones)
    own_state = (augmented(widen(own_g[:K])), ones)
    for k in range(2 * K):
        state = eliminate(state, k)
        if k < K:
            own_state = eliminate(own_state, k)
    own_inverse = own_state[0][:, K : 2 * K]
    inverse_32 = state[0][:, 2 * K : 4 * K]
    change_hi, change_lo = split(changes)
    change_both = jnp.concatenate([change_hi, change_lo], 0)
    product = nn(change_both, mhi[...])
    product = product[: 2 * K] + product[2 * K :] + nn(change_hi, mlo[...])
    solved = nn(inverse_32, product, HIGH)
    solved_hi, solved_lo = split(solved)
    scat[...] = jnp.concatenate(
        [solved_hi, solved_hi, solved_lo, jnp.zeros((2 * K, ne), BF16)], 0
    )
    first_rows = diagonals(nn(own_g[K:], own_inverse, HIGH))
    next_rows = diagonals(nn(ratio_g[2 * K :], inverse_32[:, K:], HIGH))
    for update, rows in enumerate((first_rows, next_rows)):
        for a in range(3):
            drift[3 * update + a] = rows[a]
        lap[update] = rows[3]
    logs = jnp.sum(jnp.log(jnp.abs(state[1])), 1, keepdims=True)
    weight[...] = known["log"][0:1, 0:1] + logs

    for copy in y_copies + packets + list(z_copies.values()) + list(s_copies.values()):
        copy.wait_send()
    for copies in x_copies.values():
        for copy in copies:
            copy.wait_send()


def finish_kernel(chosen, ccat, scat, drift_in, lap_in, weight_in,
                  out, drift, lap, weight, rows_f, sems):
    parts = sems.shape[0]
    size = chosen.shape[0] // parts
    copies = []
    for i in range(parts):
        rows = pl.ds(i * size, size)
        change = nn(ccat[rows], scat[...])
        rows_f[rows] = chosen[rows] - change
        copies.append(pltpu.make_async_copy(rows_f.at[rows], out.at[0, rows], sems.at[i]))
        copies[-1].start()
    drift[...] = drift_in[...]
    lap[...] = lap_in[...]
    weight[...] = weight_in[...]
    for copy in copies:
        copy.wait()


def per_device(
    wavevectors, coefficients, inverse, positions, displacements, moved, donor, take, log_weight
):
    ne = inverse.shape[1]
    npw = coefficients.shape[0]
    ng = wavevectors.shape[1]
    steps = ne // 2 // CHUNK + LAG
    laps = NY * (NZ - 1) // 2
    vmem = pl.BlockSpec(memory_space=pltpu.VMEM)
    smem = pl.BlockSpec(memory_space=pltpu.SMEM)
    hbm = pl.BlockSpec(memory_space=pltpu.HBM)
    dma = pltpu.SemaphoreType.DMA
    shape = jax.ShapeDtypeStruct
    smalls = (shape((6, 1, K), F32), shape((2, 1, K), F32), shape((1, 1), F32))
    states = pl.pallas_call(
        main_kernel,
        out_shape=(
            shape((ne, ne), F32),
            shape((ne, 128), BF16),
            shape((128, ne), BF16),
        )
        + smalls,
        in_specs=[smem] * 3 + [hbm] * 6,
        out_specs=(vmem,) * 6,
        scratch_shapes=[
            pltpu.VMEM((ne, ne), F32),
            pltpu.VMEM((ne, ne), BF16),
            pltpu.VMEM((ne, ne), BF16),
            pltpu.VMEM((NZ * NY, 2, K, npw), BF16),
            pltpu.VMEM((2, steps, CHUNK, ne), BF16),
            pltpu.VMEM((2, steps, CHUNK, ne), BF16),
            pltpu.VMEM((3, ng), F32),
            pltpu.VMEM((NX, 3, 1, ne), F32),
            pltpu.VMEM((NX, 6, 1, K), F32),
            pltpu.VMEM((NX, 2, 1, K), jnp.int32),
            pltpu.VMEM((NX, 8, 128), F32),
            pltpu.VMEM((14 * K, npw), BF16),
            pltpu.VMEM((14 * K, ne), F32),
            pltpu.VMEM((ne, 128), BF16),
            dma((8,)),
            dma((5,)),
            dma((NY - 1,)),
            dma((NY - 1,)),
            dma((NX - 1, 4)),
            dma((NX - 1, 4)),
            dma((2, steps)),
            dma((2, steps)),
            dma((2, laps)),
            dma((2, laps)),
            dma((NY + 2 * laps,)),
            dma((NY + 2 * laps,)),
        ],
        compiler_params=pltpu.CompilerParams(
            collective_id=0, has_side_effects=True, vmem_limit_bytes=40 << 20
        ),
        name="exchange_and_update",
    )(
        donor,
        take,
        log_weight,
        *(
            pltpu.with_memory_space_constraint(x, pltpu.HBM)
            for x in (
                wavevectors,
                positions.transpose(1, 0, 2),
                displacements.reshape(6, 1, K),
                moved,
                coefficients.T,
                inverse,
            )
        ),
    )
    result, drift, lap, weight = pl.pallas_call(
        finish_kernel,
        out_shape=(shape((1, ne, ne), F32),) + smalls,
        in_specs=[vmem] * 6,
        out_specs=(hbm,) + (vmem,) * 3,
        scratch_shapes=[pltpu.VMEM((ne, ne), F32), dma((8,))],
        compiler_params=pltpu.CompilerParams(vmem_limit_bytes=16 << 20),
        name="rank_update",
    )(*states)
    return (result, drift.reshape(2, 1, 3, K), lap, weight.reshape(1))


def solution(mesh):
    return jax.shard_map(
        per_device,
        mesh=mesh,
        in_specs=(
            P(),
            P(None, "orb"),
            P(("grp", "orb"), None, None),
            P(("grp", "orb"), None, None),
            P(None, ("grp", "orb"), None, None),
            P(None, ("grp", "orb"), None),
            P("orb"),
            P(("grp", "orb")),
            P(("grp", "orb")),
        ),
        out_specs=(
            P(("grp", "orb"), None, None),
            P(None, ("grp", "orb"), None, None),
            P(None, ("grp", "orb"), None),
            P(("grp", "orb")),
        ),
        check_vma=False,
    )
```

```python
import jax
import jax.numpy as jnp
from jax import lax
from jax.experimental import pallas as pl
from jax.experimental.pallas import tpu as pltpu
from jax.sharding import PartitionSpec as P

F32 = jnp.float32
BF16 = jnp.bfloat16
NX, NY, NZ = 4, 4, 8
LAG = 6
VALUE_STEPS = (23, 30, 37)
CHUNK = 16
K = 16
HIGH = lax.Precision.HIGHEST
MESH = pl.DeviceIdType.MESH


def nn(a, b, precision=None):
    return lax.dot_general(
        a, b, (((1,), (0,)), ((), ())), precision=precision, preferred_element_type=F32
    )


def nt(a, b):
    return lax.dot_general(a, b, (((1,), (1,)), ((), ())), preferred_element_type=F32)


def split(a):
    hi = a.astype(BF16)
    return hi, (a - hi.astype(F32)).astype(BF16)


def iota(shape, dim):
    return lax.broadcasted_iota(jnp.int32, shape, dim)


def column(row):
    return jnp.sum(jnp.where(iota((K, K), 0) == iota((K, K), 1), row, 0.0), 1, keepdims=True)


def one_hot(indices, width):
    return jnp.where(iota((K, width), 1) == indices.astype(jnp.int32), 1.0, 0.0)


def pick(hot, row):
    return jnp.sum(hot * row, 1, keepdims=True)


def eliminate(state, k):
    a, pivots = state
    row = iota(a.shape, 0)
    col = jnp.broadcast_to(a[:, k : k + 1], a.shape)
    size = jnp.abs(col)
    scaled = size * 257.0
    key = (scaled - (scaled - size)) * (1.0 + row.astype(F32) * 2.0**-22)
    key = jnp.where(row >= k, key, -1.0)
    chosen = key == jnp.max(key, 0, keepdims=True)
    pivot_row = jnp.sum(jnp.where(chosen, a, 0.0), 0, keepdims=True)
    pivot = jnp.sum(jnp.where(chosen, col, 0.0), 0, keepdims=True)
    other = jnp.where(chosen, a[k : k + 1], a)
    factor = jnp.where(chosen, col[k : k + 1], col)
    pivot_row = pivot_row * (1.0 / pivot)
    a = jnp.where(row == k, pivot_row, other - factor * pivot_row)
    pivots = jnp.where(iota(pivots.shape, 1) == k, pivot, pivots)
    return a, pivots


def augmented(x):
    n = x.shape[0]
    r, c = iota(x.shape, 0), iota(x.shape, 1)
    return jnp.where(c < n, x, 0.0) + jnp.where((c == r) | (c == r + n), 1.0, 0.0)


def wave_rows(points, kvec):
    phases = points[0] * kvec[0:1] + points[1] * kvec[1:2]
    phases = phases + points[2] * kvec[2:3]
    return jnp.cos(phases).astype(BF16), jnp.sin(phases).astype(BF16)


def slope_rows(waves, kvec):
    cos, sin = waves[0].astype(F32), waves[1].astype(F32)
    rows = []
    for a in range(3):
        k = kvec[a : a + 1]
        rows.append(((-k * sin).astype(BF16), (k * cos).astype(BF16)))
    square = kvec[0:1] * kvec[0:1] + kvec[1:2] * kvec[1:2] + kvec[2:3] * kvec[2:3]
    rows.append(((-square * cos).astype(BF16), (-square * sin).astype(BF16)))
    return rows


def diagonals(block):
    eye = iota((K, K), 0) == iota((K, K), 1)
    return [
        jnp.sum(jnp.where(eye, block[K * i : K * (i + 1)], 0.0), 0, keepdims=True)
        for i in range(4)
    ]


def main_kernel(
    donor, take, log_weight, kvec_in, pos_in, disp_in, moved_in, coef, inverse,
    chosen, ccat, scat, rest_out,
    mf, mhi, mlo, cbuf, sx, rx, kvec, pk_pos, pk_disp, pk_moved, pk_log, waves, values, cown,
    m_sem, c_sem, y_send, y_recv, p_send, p_recv, x_send, x_recv,
    z_send, z_recv, s_send, s_recv,
):
    ne, ng = mf.shape[0], kvec.shape[1]
    steps = rx.shape[1]
    total = ne // CHUNK
    g = lax.axis_index("grp")
    o = lax.axis_index("orb")
    core, y, z = lax.rem(o, 2), lax.rem(o // 2, NY), o // (2 * NY)

    def orb(zz, yy, cc):
        return (zz * NY + yy) * 2 + cc

    def turn(value, by, size):
        return lax.rem(value + by + size, size)

    def remote(src, dst, send, recv, grp, orb_index):
        return pltpu.make_async_remote_copy(
            src_ref=src, dst_ref=dst, send_sem=send, recv_sem=recv,
            device_id=(grp, orb_index), device_id_type=MESH,
        )

    def shard(zz, yy, cc=core):
        return cbuf.at[zz * NY + yy, cc]

    barrier = pltpu.get_barrier_semaphore()
    up, down = orb(turn(z, 1, NZ), y, core), orb(turn(z, -1, NZ), y, core)
    sibling = orb(z, y, 1 - core)
    partners = [(turn(g, d, NX), o) for d in range(1, NX)]
    partners += [(g, orb(z, turn(y, d, NY), core)) for d in range(1, NY)]
    partners += [(g, up), (g, down), (g, sibling)]
    for partner in partners:
        pl.semaphore_signal(barrier, inc=1, device_id=partner, device_id_type=MESH)

    pieces = m_sem.shape[0]
    piece = ne // pieces
    loads = []
    for i in range(pieces):
        rows = pl.ds(i * piece, piece)
        loads.append(pltpu.make_async_copy(inverse.at[0, rows], mf.at[rows], m_sem.at[i]))
    for i in range(pieces // 2):
        loads[i].start()
        loads[pieces - 1 - i].start()
    small = [
        pltpu.make_async_copy(src, dst, c_sem.at[i])
        for i, (src, dst) in enumerate(
            (
                (kvec_in, kvec),
                (pos_in, pk_pos.at[g]),
                (disp_in, pk_disp.at[g]),
                (moved_in, pk_moved.at[g]),
                (coef, shard(z, y)),
            )
        )
    ]
    for copy in small:
        copy.start()
    pk_log[g] = jnp.full((8, 128), log_weight[0], F32)
    pl.semaphore_wait(barrier, len(partners))

    is_source = donor[0] == g
    right, left = turn(g, 1, NX), turn(g, -1, NX)
    x_copies = {}

    def x_arrived(t):
        for copy in x_copies[t]:
            copy.wait_recv()

    def x_step(t):
        if t >= LAG:
            x_arrived(t - LAG)
        for way, first in ((0, t * CHUNK), (1, ne - (t + 1) * CHUNK)):
            own = mf[first : first + CHUNK].astype(BF16)
            sx[way, t] = jnp.where(is_source, own, rx[way, t - LAG]) if t >= LAG else own
        x_copies[t] = [
            remote(sx.at[way, t], rx.at[way, t], x_send.at[way, t], x_recv.at[way, t], to, o)
            for way, to in ((0, right), (1, left))
        ]
        for copy in x_copies[t]:
            copy.start()

    taking = jnp.logical_and(take[0] == 1, donor[0] != g)
    ahead = lax.rem(g - donor[0] + NX, NX)

    def places_of(r):
        found = []
        for hops in range(1, NX):
            t = r + (hops - 1) * LAG
            if t < steps:
                found.append((0, t))
            else:
                found.append((1, total - 1 - r + (NX - hops - 1) * LAG))
        return found

    ready = {}
    for r in range(total):
        ready.setdefault(max(t for _, t in places_of(r)), []).append(r)

    def select(r):
        rows = pl.ds(r * CHUNK, CHUNK)
        hi, lo = split(mf[rows])
        one, two, three = (rx[way, t] for way, t in places_of(r))
        got = jnp.where(ahead == 1, one, jnp.where(ahead == 2, two, three))
        mhi[rows] = jnp.where(taking, got, hi)
        mlo[rows] = jnp.where(taking, jnp.zeros_like(lo), lo)
        chosen[rows] = jnp.where(taking, got.astype(F32), mf[rows])

    y_copies = [
        remote(coef, shard(z, y), y_send.at[d - 1], y_recv.at[d - 1], g,
               orb(z, turn(y, d, NY), core))
        for d in range(1, NY)
    ]
    laps = NY * (NZ - 1) // 2
    full = NY * (NZ // 2 - 1)
    rest = laps - full
    z_copies, s_copies, seen = {}, {}, set()

    def item(way, k):
        if k < full:
            return k // NY, k % NY
        return NZ // 2 - 1, k - full + (rest if way else 0)

    def place(way, m, j):
        return shard(turn(z, m if way else -m, NZ), turn(y, j, NY))

    def to_sibling(index, src, dst):
        s_copies[index] = remote(src, dst, s_send.at[index], s_recv.at[index], g, sibling)
        s_copies[index].start()

    def z_arrived(way, k):
        if (way, k) not in seen:
            seen.add((way, k))
            z_copies[way, k].wait_recv()
            m, j = item(way, k)
            got = place(way, m + 1, j)
            to_sibling(NY + way * laps + k, got, got)

    def z_step(k):
        if k < laps:
            for way in range(2):
                m, j = item(way, k)
                src = dst = place(way, m, j)
                if m:
                    z_arrived(way, k - NY if k < full else full - NY + j)
                elif j == 0:
                    src = coef
                elif way == 0:
                    y_copies[NY - j - 1].wait_recv()
                z_copies[way, k] = remote(
                    src, dst, z_send.at[way, k], z_recv.at[way, k], g, (up, down)[way]
                )
                z_copies[way, k].start()
                if m == 0 and way == 0:
                    to_sibling(j, src, dst)
        if k >= NY:
            for way in range(2):
                z_arrived(way, k - NY)

    packets = []
    for d in range(1, NX):
        for i, (src, all_slots) in enumerate(
            ((pos_in, pk_pos), (disp_in, pk_disp), (moved_in, pk_moved), (pk_log.at[g], pk_log))
        ):
            packets.append(
                remote(src, all_slots.at[g], p_send.at[d - 1, i], p_recv.at[d - 1, i],
                       turn(g, d, NX), o)
            )
    known = {}

    def find_points():
        for copy in packets:
            copy.wait_recv()
        for copy in small:
            copy.wait()
        parent = jnp.where(taking, donor[0], g)
        hot_own = one_hot(column(pk_moved[g, 0].astype(F32)), ne)
        hot_par = one_hot(column(pk_moved[parent, 0].astype(F32)), ne)
        hot_next = one_hot(column(pk_moved[g, 1].astype(F32)), ne)
        old_own = [pick(hot_own, pk_pos[g, a]) for a in range(3)]
        new_own = [old_own[a] + column(pk_disp[g, a]) for a in range(3)]
        old_par = [pick(hot_par, pk_pos[parent, a]) for a in range(3)]
        new_par = [old_par[a] + column(pk_disp[parent, a]) for a in range(3)]
        was_moved = jnp.sum(hot_par, 0, keepdims=True) > 0.0
        old_next = []
        for a in range(3):
            placed = jnp.sum(hot_par * new_par[a], 0, keepdims=True)
            old_next.append(pick(hot_next, jnp.where(was_moved, placed, pk_pos[parent, a])))
        new_next = [old_next[a] + column(pk_disp[g, 3 + a]) for a in range(3)]
        known["points"] = (old_own, old_par, new_par, old_next, new_own, new_next)
        zeros = jnp.zeros((2 * K, ne), F32)
        pair = jnp.concatenate([hot_par, hot_next], 0)
        known["hi"] = jnp.concatenate([pair, zeros, pair, zeros], 0).astype(BF16)
        known["lo"] = jnp.concatenate([zeros, pair, zeros, zeros], 0).astype(BF16)
        wide = jnp.zeros((128 - 2 * K, ne), F32)
        none = jnp.zeros((K, ne), F32)
        known["own_hi"] = jnp.concatenate([hot_own, none, wide], 0).astype(BF16)
        known["own_lo"] = jnp.concatenate([none, hot_own, wide], 0).astype(BF16)
        known["log"] = pk_log[parent]

    def find_waves(i):
        pair = wave_rows(known["points"][i], kvec[...])
        first = i * K if i < 4 else 4 * K + (i - 4) * 5 * K
        rows = [pair] + (slope_rows(pair, kvec[...]) if i >= 4 else [])
        for n, (cos, sin) in enumerate(rows):
            waves[first + n * K : first + (n + 1) * K, :ng] = cos
            waves[first + n * K : first + (n + 1) * K, ng:] = sin

    block = 2 * NY * K

    def find_values(m):
        ends = [turn(z, m + 1, NZ), turn(z, -m, NZ)]
        table = jnp.concatenate(
            [cbuf[pl.ds(e * NY, NY)].reshape(block, cbuf.shape[3]) for e in ends], 0
        )
        result = nt(waves[...], table)
        for i, e in enumerate(ends):
            lanes = pl.ds(pl.multiple_of(e * block, block), block)
            values[:, lanes] = result[:, i * block : (i + 1) * block]

    def s_wait(m):
        for way in range(2):
            for k in range(laps):
                offset = item(way, k)[0] + 1
                if offset == (m + 1 if way else m) or offset == m + 1 == NZ // 2:
                    s_copies[NY + way * laps + k].wait_recv()
        if m == 0:
            for j in range(NY):
                s_copies[j].wait_recv()

    tile = min(256, ne)

    def own_columns(i):
        rows = pl.ds(i * tile, tile)
        hi, lo = split(mf[rows])
        cown[rows] = (nt(hi, known["own_hi"]) + nt(lo, known["own_lo"])).astype(BF16)

    def columns(i):
        rows = pl.ds(i * tile, tile)
        ccat[rows] = (nt(mhi[rows], known["hi"]) + nt(mlo[rows], known["lo"])).astype(BF16)

    tiles = ne // tile
    work = {}

    def plan(t, what, *args):
        work.setdefault(min(t, steps - 1), []).append((what, args))

    plan(8, find_points)
    for i in range(6):
        plan(9 + i, find_waves, i)
    for i in range(tiles):
        plan(15 + i, own_columns, i)
    early = [i for i in (0, tiles - 1) if tiles > 2]
    for i in early:
        plan(steps - 3 + (i > 0), columns, i)
    for m in range(NZ // 2 - 1):
        plan(VALUE_STEPS[m], lambda m: (s_wait(m), find_values(m)), m)

    for t in range(steps):
        for i in range(pieces // 2):
            if t == 2 * i:
                loads[i].wait()
                loads[pieces - 1 - i].wait()
        x_step(t)
        if t == 0:
            for copy in y_copies + packets:
                copy.start()
        if t >= LAG:
            for r in ready.get(t - LAG, ()):
                select(r)
        for k in range(laps + NY):
            if t == (min(2 * k + 4, steps - 1) if k else 0):
                z_step(k)
        for what, args in work.get(t, ()):
            what(*args)
    for t in range(steps - LAG, steps):
        x_arrived(t)
        for r in ready.get(t, ()):
            select(r)
    for i in range(tiles):
        if i not in early:
            columns(i)
    s_wait(NZ // 2 - 1)
    find_values(NZ // 2 - 1)

    def stacked(rows):
        hi, lo = split(rows)
        return jnp.concatenate([hi, lo], 0)

    base, second = 4 * K, 9 * K
    own_left = stacked(
        jnp.concatenate([values[base : base + K] - values[0:K], values[base + K : second]], 0)
    )
    changes = jnp.concatenate(
        [values[2 * K : 3 * K] - values[K : 2 * K], values[second : second + K] - values[3 * K : base]], 0
    )
    slopes = values[second + K :]
    left = stacked(jnp.concatenate([changes, slopes], 0))
    cut = own_left.shape[0] // 2
    own_got = nn(own_left, cown[...])
    own_g = own_got[:cut] + own_got[cut:]
    own_g = own_g[:, :K] + own_got[:cut, K : 2 * K]
    cut = left.shape[0] // 2
    got = nn(left, ccat[...])
    lanes = got[:cut] + got[cut:]
    ratio_g = lanes[:, : 2 * K] + got[:cut, 2 * K : 4 * K]

    def widen(x):
        return jnp.concatenate([x, jnp.zeros((x.shape[0], 128 - x.shape[1]), F32)], 1)

    state = (augmented(widen(ratio_g[: 2 * K])), jnp.ones((1, 128), F32))
    for k in range(2 * K):
        state = eliminate(state, k)
    inverse_32 = state[0][:, 2 * K : 4 * K]
    change_hi, change_lo = split(changes)
    change_both = jnp.concatenate([change_hi, change_lo], 0)
    product = nn(change_both, mhi[...])
    product = product[: 2 * K] + product[2 * K :] + nn(change_hi, mlo[...])
    product_hi, product_lo = split(product)
    inverse_both = stacked(inverse_32)
    solved = nn(inverse_both, product_hi)
    solved = solved[: 2 * K] + solved[2 * K :] + nn(inverse_both[: 2 * K], product_lo)
    solved_hi, solved_lo = split(solved)
    scat[...] = jnp.concatenate(
        [solved_hi, solved_hi, solved_lo, jnp.zeros((2 * K, ne), BF16)], 0
    )
    rest_out[0 : 5 * K] = widen(own_g)
    rest_out[5 * K : 9 * K] = widen(ratio_g[2 * K :])
    rest_out[9 * K : 11 * K] = widen(inverse_32)
    rest_out[11 * K : 11 * K + 8] = jnp.broadcast_to(state[1], (8, 128))
    rest_out[11 * K + 8 :] = known["log"]

    for copy in y_copies + packets + list(z_copies.values()) + list(s_copies.values()):
        copy.wait_send()
    for copies in x_copies.values():
        for copy in copies:
            copy.wait_send()


def finish_kernel(chosen, ccat, scat, rest_in, out, drift, lap, weight, rows_f, sems):
    parts = sems.shape[0]
    size = chosen.shape[0] // parts
    copies = []
    for i in range(parts):
        rows = pl.ds(i * size, size)
        rows_f[rows] = chosen[rows] - nn(ccat[rows], scat[...])
        copies.append(pltpu.make_async_copy(rows_f.at[rows], out.at[0, rows], sems.at[i]))
        copies[-1].start()
    own_state = (augmented(rest_in[0:K]), jnp.ones((1, 128), F32))
    for k in range(K):
        own_state = eliminate(own_state, k)
    own_inverse = own_state[0][:, K : 2 * K]
    inverse_32 = rest_in[9 * K : 11 * K, : 2 * K]
    first = diagonals(nn(rest_in[K : 5 * K, :K], own_inverse, HIGH))
    second = diagonals(nn(rest_in[5 * K : 9 * K, : 2 * K], inverse_32[:, K:], HIGH))
    for update, rows in enumerate((first, second)):
        for a in range(3):
            drift[3 * update + a] = rows[a]
        lap[update] = rows[3]
    logs = jnp.sum(jnp.log(jnp.abs(rest_in[11 * K : 11 * K + 1])), 1, keepdims=True)
    weight[...] = rest_in[11 * K + 8 : 11 * K + 9, 0:1] + logs
    for copy in copies:
        copy.wait()


def per_device(
    wavevectors, coefficients, inverse, positions, displacements, moved, donor, take, log_weight
):
    ne = inverse.shape[1]
    npw = coefficients.shape[0]
    ng = wavevectors.shape[1]
    steps = ne // 2 // CHUNK + LAG
    laps = NY * (NZ - 1) // 2
    vmem = pl.BlockSpec(memory_space=pltpu.VMEM)
    smem = pl.BlockSpec(memory_space=pltpu.SMEM)
    hbm = pl.BlockSpec(memory_space=pltpu.HBM)
    dma = pltpu.SemaphoreType.DMA
    shape = jax.ShapeDtypeStruct
    smalls = (shape((6, 1, K), F32), shape((2, 1, K), F32), shape((1, 1), F32))
    states = pl.pallas_call(
        main_kernel,
        out_shape=(
            shape((ne, ne), F32),
            shape((ne, 128), BF16),
            shape((128, ne), BF16),
            shape((12 * K, 128), F32),
        ),
        in_specs=[smem] * 3 + [hbm] * 6,
        out_specs=(vmem,) * 4,
        scratch_shapes=[
            pltpu.VMEM((ne, ne), F32),
            pltpu.VMEM((ne, ne), BF16),
            pltpu.VMEM((ne, ne), BF16),
            pltpu.VMEM((NZ * NY, 2, K, npw), BF16),
            pltpu.VMEM((2, steps, CHUNK, ne), BF16),
            pltpu.VMEM((2, steps, CHUNK, ne), BF16),
            pltpu.VMEM((3, ng), F32),
            pltpu.VMEM((NX, 3, 1, ne), F32),
            pltpu.VMEM((NX, 6, 1, K), F32),
            pltpu.VMEM((NX, 2, 1, K), jnp.int32),
            pltpu.VMEM((NX, 8, 128), F32),
            pltpu.VMEM((14 * K, npw), BF16),
            pltpu.VMEM((14 * K, ne), F32),
            pltpu.VMEM((ne, 128), BF16),
            dma((8,)),
            dma((5,)),
            dma((NY - 1,)),
            dma((NY - 1,)),
            dma((NX - 1, 4)),
            dma((NX - 1, 4)),
            dma((2, steps)),
            dma((2, steps)),
            dma((2, laps)),
            dma((2, laps)),
            dma((NY + 2 * laps,)),
            dma((NY + 2 * laps,)),
        ],
        compiler_params=pltpu.CompilerParams(
            collective_id=0, has_side_effects=True, vmem_limit_bytes=40 << 20
        ),
        name="exchange_and_update",
    )(
        donor,
        take,
        log_weight,
        *(
            pltpu.with_memory_space_constraint(x, pltpu.HBM)
            for x in (
                wavevectors,
                positions.transpose(1, 0, 2),
                displacements.reshape(6, 1, K),
                moved,
                coefficients.T,
                inverse,
            )
        ),
    )
    result, drift, lap, weight = pl.pallas_call(
        finish_kernel,
        out_shape=(shape((1, ne, ne), F32),) + smalls,
        in_specs=[vmem] * 4,
        out_specs=(hbm,) + (vmem,) * 3,
        scratch_shapes=[pltpu.VMEM((ne, ne), F32), dma((8,))],
        compiler_params=pltpu.CompilerParams(vmem_limit_bytes=16 << 20),
        name="rank_update",
    )(*states)
    return (result, drift.reshape(2, 1, 3, K), lap, weight.reshape(1))


def solution(mesh):
    return jax.shard_map(
        per_device,
        mesh=mesh,
        in_specs=(
            P(),
            P(None, "orb"),
            P(("grp", "orb"), None, None),
            P(("grp", "orb"), None, None),
            P(None, ("grp", "orb"), None, None),
            P(None, ("grp", "orb"), None),
            P("orb"),
            P(("grp", "orb")),
            P(("grp", "orb")),
        ),
        out_specs=(
            P(("grp", "orb"), None, None),
            P(None, ("grp", "orb"), None, None),
            P(None, ("grp", "orb"), None),
            P(("grp", "orb")),
        ),
        check_vma=False,
    )
```

```python
import jax
import jax.numpy as jnp
from jax import lax
from jax.experimental import pallas as pl
from jax.experimental.pallas import tpu as pltpu
from jax.sharding import PartitionSpec as P

F32 = jnp.float32
BF16 = jnp.bfloat16
NX, NY, NZ = 4, 4, 8
LAG = 6
VALUE_STEPS = (23, 30, 37)
CHUNK = 16
K = 16
HIGH = lax.Precision.HIGHEST
MESH = pl.DeviceIdType.MESH


def nn(a, b, precision=None):
    return lax.dot_general(
        a, b, (((1,), (0,)), ((), ())), precision=precision, preferred_element_type=F32
    )


def nt(a, b):
    return lax.dot_general(a, b, (((1,), (1,)), ((), ())), preferred_element_type=F32)


def split(a):
    hi = a.astype(BF16)
    return hi, (a - hi.astype(F32)).astype(BF16)


def iota(shape, dim):
    return lax.broadcasted_iota(jnp.int32, shape, dim)


def column(row):
    return jnp.sum(jnp.where(iota((K, K), 0) == iota((K, K), 1), row, 0.0), 1, keepdims=True)


def one_hot(indices, width):
    return jnp.where(iota((K, width), 1) == indices.astype(jnp.int32), 1.0, 0.0)


def pick(hot, row):
    return jnp.sum(hot * row, 1, keepdims=True)


def start(ratio):
    a = augmented(ratio)
    return a, jnp.ones((1, 128), F32), jnp.broadcast_to(a[:, 0:1], a.shape)


def eliminate(state, k):
    a, pivots, col = state
    row = iota(a.shape, 0)
    after = jnp.broadcast_to(a[:, k + 1 : k + 2], a.shape)
    size = jnp.abs(col)
    scaled = size * 257.0
    key = (scaled - (scaled - size)) * (1.0 + row.astype(F32) * 2.0**-22)
    key = jnp.where(row >= k, key, -1.0)
    chosen = key == jnp.max(key, 0, keepdims=True)

    def chosen_row(x):
        return jnp.sum(jnp.where(chosen, x, 0.0), 0, keepdims=True)

    pivot = chosen_row(col)
    factor = jnp.where(chosen, col[k : k + 1], col)
    scale = 1.0 / pivot

    def update(x):
        pivot_row = chosen_row(x) * scale
        return jnp.where(row == k, pivot_row, jnp.where(chosen, x[k : k + 1], x) - factor * pivot_row)

    pivots = jnp.where(iota(pivots.shape, 1) == k, pivot, pivots)
    return update(a), pivots, update(after)


def augmented(x):
    n = x.shape[0]
    r, c = iota(x.shape, 0), iota(x.shape, 1)
    return jnp.where(c < n, x, 0.0) + jnp.where((c == r) | (c == r + n), 1.0, 0.0)


def wave_rows(points, kvec):
    phases = points[0] * kvec[0:1] + points[1] * kvec[1:2]
    phases = phases + points[2] * kvec[2:3]
    return jnp.cos(phases).astype(BF16), jnp.sin(phases).astype(BF16)


def slope_rows(waves, kvec):
    cos, sin = waves[0].astype(F32), waves[1].astype(F32)
    rows = []
    for a in range(3):
        k = kvec[a : a + 1]
        rows.append(((-k * sin).astype(BF16), (k * cos).astype(BF16)))
    square = kvec[0:1] * kvec[0:1] + kvec[1:2] * kvec[1:2] + kvec[2:3] * kvec[2:3]
    rows.append(((-square * cos).astype(BF16), (-square * sin).astype(BF16)))
    return rows


def diagonals(block):
    eye = iota((K, K), 0) == iota((K, K), 1)
    return [
        jnp.sum(jnp.where(eye, block[K * i : K * (i + 1)], 0.0), 0, keepdims=True)
        for i in range(4)
    ]


def main_kernel(
    donor, take, log_weight, kvec_in, pos_in, disp_in, moved_in, coef, inverse,
    chosen, ccat, scat, rest_out,
    mf, mhi, mlo, cbuf, sx, rx, kvec, pk_pos, pk_disp, pk_moved, pk_log, waves, values, cown,
    m_sem, c_sem, y_send, y_recv, p_send, p_recv, x_send, x_recv,
    z_send, z_recv, s_send, s_recv,
):
    ne, ng = mf.shape[0], kvec.shape[1]
    steps = rx.shape[1]
    total = ne // CHUNK
    g = lax.axis_index("grp")
    o = lax.axis_index("orb")
    core, y, z = lax.rem(o, 2), lax.rem(o // 2, NY), o // (2 * NY)

    def orb(zz, yy, cc):
        return (zz * NY + yy) * 2 + cc

    def turn(value, by, size):
        return lax.rem(value + by + size, size)

    def remote(src, dst, send, recv, grp, orb_index):
        return pltpu.make_async_remote_copy(
            src_ref=src, dst_ref=dst, send_sem=send, recv_sem=recv,
            device_id=(grp, orb_index), device_id_type=MESH,
        )

    def shard(zz, yy, cc=core):
        return cbuf.at[zz * NY + yy, cc]

    barrier = pltpu.get_barrier_semaphore()
    up, down = orb(turn(z, 1, NZ), y, core), orb(turn(z, -1, NZ), y, core)
    sibling = orb(z, y, 1 - core)
    partners = [(turn(g, d, NX), o) for d in range(1, NX)]
    partners += [(g, orb(z, turn(y, d, NY), core)) for d in range(1, NY)]
    partners += [(g, up), (g, down), (g, sibling)]
    for partner in partners:
        pl.semaphore_signal(barrier, inc=1, device_id=partner, device_id_type=MESH)

    pieces = m_sem.shape[0]
    piece = ne // pieces
    loads = []
    for i in range(pieces):
        rows = pl.ds(i * piece, piece)
        loads.append(pltpu.make_async_copy(inverse.at[0, rows], mf.at[rows], m_sem.at[i]))
    for i in range(pieces // 2):
        loads[i].start()
        loads[pieces - 1 - i].start()
    small = [
        pltpu.make_async_copy(src, dst, c_sem.at[i])
        for i, (src, dst) in enumerate(
            (
                (kvec_in, kvec),
                (pos_in, pk_pos.at[g]),
                (disp_in, pk_disp.at[g]),
                (moved_in, pk_moved.at[g]),
                (coef, shard(z, y)),
            )
        )
    ]
    for copy in small:
        copy.start()
    pk_log[g] = jnp.full((8, 128), log_weight[0], F32)
    pl.semaphore_wait(barrier, len(partners))

    is_source = donor[0] == g
    right, left = turn(g, 1, NX), turn(g, -1, NX)
    x_copies = {}

    def x_arrived(t):
        for copy in x_copies[t]:
            copy.wait_recv()

    def x_step(t):
        if t >= LAG:
            x_arrived(t - LAG)
        for way, first in ((0, t * CHUNK), (1, ne - (t + 1) * CHUNK)):
            own = mf[first : first + CHUNK].astype(BF16)
            sx[way, t] = jnp.where(is_source, own, rx[way, t - LAG]) if t >= LAG else own
        x_copies[t] = [
            remote(sx.at[way, t], rx.at[way, t], x_send.at[way, t], x_recv.at[way, t], to, o)
            for way, to in ((0, right), (1, left))
        ]
        for copy in x_copies[t]:
            copy.start()

    taking = jnp.logical_and(take[0] == 1, donor[0] != g)
    ahead = lax.rem(g - donor[0] + NX, NX)

    def places_of(r):
        found = []
        for hops in range(1, NX):
            t = r + (hops - 1) * LAG
            if t < steps:
                found.append((0, t))
            else:
                found.append((1, total - 1 - r + (NX - hops - 1) * LAG))
        return found

    ready = {}
    for r in range(total):
        ready.setdefault(max(t for _, t in places_of(r)), []).append(r)

    def select(r):
        rows = pl.ds(r * CHUNK, CHUNK)
        hi, lo = split(mf[rows])
        one, two, three = (rx[way, t] for way, t in places_of(r))
        got = jnp.where(ahead == 1, one, jnp.where(ahead == 2, two, three))
        mhi[rows] = jnp.where(taking, got, hi)
        mlo[rows] = jnp.where(taking, jnp.zeros_like(lo), lo)
        chosen[rows] = jnp.where(taking, got.astype(F32), mf[rows])

    y_copies = [
        remote(coef, shard(z, y), y_send.at[d - 1], y_recv.at[d - 1], g,
               orb(z, turn(y, d, NY), core))
        for d in range(1, NY)
    ]
    laps = NY * (NZ - 1) // 2
    full = NY * (NZ // 2 - 1)
    rest = laps - full
    z_copies, s_copies, seen = {}, {}, set()

    def item(way, k):
        if k < full:
            return k // NY, k % NY
        return NZ // 2 - 1, k - full + (rest if way else 0)

    def place(way, m, j):
        return shard(turn(z, m if way else -m, NZ), turn(y, j, NY))

    def to_sibling(index, src, dst):
        s_copies[index] = remote(src, dst, s_send.at[index], s_recv.at[index], g, sibling)
        s_copies[index].start()

    def z_arrived(way, k):
        if (way, k) not in seen:
            seen.add((way, k))
            z_copies[way, k].wait_recv()
            m, j = item(way, k)
            got = place(way, m + 1, j)
            to_sibling(NY + way * laps + k, got, got)

    def z_step(k):
        if k < laps:
            for way in range(2):
                m, j = item(way, k)
                src = dst = place(way, m, j)
                if m:
                    z_arrived(way, k - NY if k < full else full - NY + j)
                elif j == 0:
                    src = coef
                elif way == 0:
                    y_copies[NY - j - 1].wait_recv()
                z_copies[way, k] = remote(
                    src, dst, z_send.at[way, k], z_recv.at[way, k], g, (up, down)[way]
                )
                z_copies[way, k].start()
                if m == 0 and way == 0:
                    to_sibling(j, src, dst)
        if k >= NY:
            for way in range(2):
                z_arrived(way, k - NY)

    packets = []
    for d in range(1, NX):
        for i, (src, all_slots) in enumerate(
            ((pos_in, pk_pos), (disp_in, pk_disp), (moved_in, pk_moved), (pk_log.at[g], pk_log))
        ):
            packets.append(
                remote(src, all_slots.at[g], p_send.at[d - 1, i], p_recv.at[d - 1, i],
                       turn(g, d, NX), o)
            )
    known = {}

    def find_points():
        for copy in packets:
            copy.wait_recv()
        for copy in small:
            copy.wait()
        parent = jnp.where(taking, donor[0], g)
        hot_own = one_hot(column(pk_moved[g, 0].astype(F32)), ne)
        hot_par = one_hot(column(pk_moved[parent, 0].astype(F32)), ne)
        hot_next = one_hot(column(pk_moved[g, 1].astype(F32)), ne)
        old_own = [pick(hot_own, pk_pos[g, a]) for a in range(3)]
        new_own = [old_own[a] + column(pk_disp[g, a]) for a in range(3)]
        old_par = [pick(hot_par, pk_pos[parent, a]) for a in range(3)]
        new_par = [old_par[a] + column(pk_disp[parent, a]) for a in range(3)]
        was_moved = jnp.sum(hot_par, 0, keepdims=True) > 0.0
        old_next = []
        for a in range(3):
            placed = jnp.sum(hot_par * new_par[a], 0, keepdims=True)
            old_next.append(pick(hot_next, jnp.where(was_moved, placed, pk_pos[parent, a])))
        new_next = [old_next[a] + column(pk_disp[g, 3 + a]) for a in range(3)]
        known["points"] = (old_own, old_par, new_par, old_next, new_own, new_next)
        zeros = jnp.zeros((2 * K, ne), F32)
        pair = jnp.concatenate([hot_par, hot_next], 0)
        known["hi"] = jnp.concatenate([pair, zeros, pair, zeros], 0).astype(BF16)
        known["lo"] = jnp.concatenate([zeros, pair, zeros, zeros], 0).astype(BF16)
        wide = jnp.zeros((128 - 2 * K, ne), F32)
        none = jnp.zeros((K, ne), F32)
        known["own_hi"] = jnp.concatenate([hot_own, none, wide], 0).astype(BF16)
        known["own_lo"] = jnp.concatenate([none, hot_own, wide], 0).astype(BF16)
        known["log"] = pk_log[parent]

    def find_waves(i):
        pair = wave_rows(known["points"][i], kvec[...])
        first = i * K if i < 4 else 4 * K + (i - 4) * 5 * K
        rows = [pair] + (slope_rows(pair, kvec[...]) if i >= 4 else [])
        for n, (cos, sin) in enumerate(rows):
            waves[first + n * K : first + (n + 1) * K, :ng] = cos
            waves[first + n * K : first + (n + 1) * K, ng:] = sin

    block = 2 * NY * K

    def find_values(m):
        ends = [turn(z, m + 1, NZ), turn(z, -m, NZ)]
        table = jnp.concatenate(
            [cbuf[pl.ds(e * NY, NY)].reshape(block, cbuf.shape[3]) for e in ends], 0
        )
        result = nt(waves[...], table)
        for i, e in enumerate(ends):
            lanes = pl.ds(pl.multiple_of(e * block, block), block)
            values[:, lanes] = result[:, i * block : (i + 1) * block]

    def s_wait(m):
        for way in range(2):
            for k in range(laps):
                offset = item(way, k)[0] + 1
                if offset == (m + 1 if way else m) or offset == m + 1 == NZ // 2:
                    s_copies[NY + way * laps + k].wait_recv()
        if m == 0:
            for j in range(NY):
                s_copies[j].wait_recv()

    tile = min(256, ne)

    def own_columns(i):
        rows = pl.ds(i * tile, tile)
        hi, lo = split(mf[rows])
        cown[rows] = (nt(hi, known["own_hi"]) + nt(lo, known["own_lo"])).astype(BF16)

    def columns(i):
        rows = pl.ds(i * tile, tile)
        ccat[rows] = (nt(mhi[rows], known["hi"]) + nt(mlo[rows], known["lo"])).astype(BF16)

    tiles = ne // tile
    work = {}

    def plan(t, what, *args):
        work.setdefault(min(t, steps - 1), []).append((what, args))

    plan(8, find_points)
    for i in range(6):
        plan(9 + i, find_waves, i)
    for i in range(tiles):
        plan(15 + i, own_columns, i)
    early = [i for i in (0, tiles - 1) if tiles > 2]
    for i in early:
        plan(steps - 3 + (i > 0), columns, i)
    for m in range(NZ // 2 - 1):
        plan(VALUE_STEPS[m], lambda m: (s_wait(m), find_values(m)), m)

    for t in range(steps):
        for i in range(pieces // 2):
            if t == 2 * i:
                loads[i].wait()
                loads[pieces - 1 - i].wait()
        x_step(t)
        if t == 0:
            for copy in y_copies + packets:
                copy.start()
        if t >= LAG:
            for r in ready.get(t - LAG, ()):
                select(r)
        for k in range(laps + NY):
            if t == (min(2 * k + 4, steps - 1) if k else 0):
                z_step(k)
        for what, args in work.get(t, ()):
            what(*args)
    for t in range(steps - LAG, steps):
        x_arrived(t)
        for r in ready.get(t, ()):
            select(r)
    for i in range(tiles):
        if i not in early:
            columns(i)
    s_wait(NZ // 2 - 1)
    find_values(NZ // 2 - 1)

    def stacked(rows):
        hi, lo = split(rows)
        return jnp.concatenate([hi, lo], 0)

    base, second = 4 * K, 9 * K
    own_left = stacked(
        jnp.concatenate([values[base : base + K] - values[0:K], values[base + K : second]], 0)
    )
    changes = jnp.concatenate(
        [values[2 * K : 3 * K] - values[K : 2 * K], values[second : second + K] - values[3 * K : base]], 0
    )
    slopes = values[second + K :]
    left = stacked(jnp.concatenate([changes, slopes], 0))
    cut = own_left.shape[0] // 2
    own_got = nn(own_left, cown[...])
    own_g = own_got[:cut] + own_got[cut:]
    own_g = own_g[:, :K] + own_got[:cut, K : 2 * K]
    cut = left.shape[0] // 2
    got = nn(left, ccat[...])
    lanes = got[:cut] + got[cut:]
    ratio_g = lanes[:, : 2 * K] + got[:cut, 2 * K : 4 * K]

    def widen(x):
        return jnp.concatenate([x, jnp.zeros((x.shape[0], 128 - x.shape[1]), F32)], 1)

    state = start(widen(ratio_g[: 2 * K]))
    for k in range(2 * K):
        state = eliminate(state, k)
    inverse_32 = state[0][:, 2 * K : 4 * K]
    change_hi, change_lo = split(changes)
    change_both = jnp.concatenate([change_hi, change_lo], 0)
    product = nn(change_both, mhi[...])
    product = product[: 2 * K] + product[2 * K :] + nn(change_hi, mlo[...])
    product_hi, product_lo = split(product)
    inverse_both = stacked(inverse_32)
    solved = nn(inverse_both, product_hi)
    solved = solved[: 2 * K] + solved[2 * K :] + nn(inverse_both[: 2 * K], product_lo)
    solved_hi, solved_lo = split(solved)
    scat[...] = jnp.concatenate(
        [solved_hi, solved_hi, solved_lo, jnp.zeros((2 * K, ne), BF16)], 0
    )
    rest_out[0 : 5 * K] = widen(own_g)
    rest_out[5 * K : 9 * K] = widen(ratio_g[2 * K :])
    rest_out[9 * K : 11 * K] = widen(inverse_32)
    rest_out[11 * K : 11 * K + 8] = jnp.broadcast_to(state[1], (8, 128))
    rest_out[11 * K + 8 :] = known["log"]

    for copy in y_copies + packets + list(z_copies.values()) + list(s_copies.values()):
        copy.wait_send()
    for copies in x_copies.values():
        for copy in copies:
            copy.wait_send()


def finish_kernel(chosen, ccat, scat, rest_in, out, drift, lap, weight, rows_f, sems):
    parts = sems.shape[0]
    size = chosen.shape[0] // parts
    copies = []
    for i in range(parts):
        rows = pl.ds(i * size, size)
        rows_f[rows] = chosen[rows] - nn(ccat[rows], scat[...])
        copies.append(pltpu.make_async_copy(rows_f.at[rows], out.at[0, rows], sems.at[i]))
        copies[-1].start()
    own_state = start(rest_in[0:K])
    for k in range(K):
        own_state = eliminate(own_state, k)
    own_inverse = own_state[0][:, K : 2 * K]
    inverse_32 = rest_in[9 * K : 11 * K, : 2 * K]
    first = diagonals(nn(rest_in[K : 5 * K, :K], own_inverse, HIGH))
    second = diagonals(nn(rest_in[5 * K : 9 * K, : 2 * K], inverse_32[:, K:], HIGH))
    for update, rows in enumerate((first, second)):
        for a in range(3):
            drift[3 * update + a] = rows[a]
        lap[update] = rows[3]
    logs = jnp.sum(jnp.log(jnp.abs(rest_in[11 * K : 11 * K + 1])), 1, keepdims=True)
    weight[...] = rest_in[11 * K + 8 : 11 * K + 9, 0:1] + logs
    for copy in copies:
        copy.wait()


def per_device(
    wavevectors, coefficients, inverse, positions, displacements, moved, donor, take, log_weight
):
    ne = inverse.shape[1]
    npw = coefficients.shape[0]
    ng = wavevectors.shape[1]
    steps = ne // 2 // CHUNK + LAG
    laps = NY * (NZ - 1) // 2
    vmem = pl.BlockSpec(memory_space=pltpu.VMEM)
    smem = pl.BlockSpec(memory_space=pltpu.SMEM)
    hbm = pl.BlockSpec(memory_space=pltpu.HBM)
    dma = pltpu.SemaphoreType.DMA
    shape = jax.ShapeDtypeStruct
    smalls = (shape((6, 1, K), F32), shape((2, 1, K), F32), shape((1, 1), F32))
    states = pl.pallas_call(
        main_kernel,
        out_shape=(
            shape((ne, ne), F32),
            shape((ne, 128), BF16),
            shape((128, ne), BF16),
            shape((12 * K, 128), F32),
        ),
        in_specs=[smem] * 3 + [hbm] * 6,
        out_specs=(vmem,) * 4,
        scratch_shapes=[
            pltpu.VMEM((ne, ne), F32),
            pltpu.VMEM((ne, ne), BF16),
            pltpu.VMEM((ne, ne), BF16),
            pltpu.VMEM((NZ * NY, 2, K, npw), BF16),
            pltpu.VMEM((2, steps, CHUNK, ne), BF16),
            pltpu.VMEM((2, steps, CHUNK, ne), BF16),
            pltpu.VMEM((3, ng), F32),
            pltpu.VMEM((NX, 3, 1, ne), F32),
            pltpu.VMEM((NX, 6, 1, K), F32),
            pltpu.VMEM((NX, 2, 1, K), jnp.int32),
            pltpu.VMEM((NX, 8, 128), F32),
            pltpu.VMEM((14 * K, npw), BF16),
            pltpu.VMEM((14 * K, ne), F32),
            pltpu.VMEM((ne, 128), BF16),
            dma((8,)),
            dma((5,)),
            dma((NY - 1,)),
            dma((NY - 1,)),
            dma((NX - 1, 4)),
            dma((NX - 1, 4)),
            dma((2, steps)),
            dma((2, steps)),
            dma((2, laps)),
            dma((2, laps)),
            dma((NY + 2 * laps,)),
            dma((NY + 2 * laps,)),
        ],
        compiler_params=pltpu.CompilerParams(
            collective_id=0, has_side_effects=True, vmem_limit_bytes=40 << 20
        ),
        name="exchange_and_update",
    )(
        donor,
        take,
        log_weight,
        *(
            pltpu.with_memory_space_constraint(x, pltpu.HBM)
            for x in (
                wavevectors,
                positions.transpose(1, 0, 2),
                displacements.reshape(6, 1, K),
                moved,
                coefficients.T,
                inverse,
            )
        ),
    )
    result, drift, lap, weight = pl.pallas_call(
        finish_kernel,
        out_shape=(shape((1, ne, ne), F32),) + smalls,
        in_specs=[vmem] * 4,
        out_specs=(hbm,) + (vmem,) * 3,
        scratch_shapes=[pltpu.VMEM((ne, ne), F32), dma((8,))],
        compiler_params=pltpu.CompilerParams(vmem_limit_bytes=16 << 20),
        name="rank_update",
    )(*states)
    return (result, drift.reshape(2, 1, 3, K), lap, weight.reshape(1))


def solution(mesh):
    return jax.shard_map(
        per_device,
        mesh=mesh,
        in_specs=(
            P(),
            P(None, "orb"),
            P(("grp", "orb"), None, None),
            P(("grp", "orb"), None, None),
            P(None, ("grp", "orb"), None, None),
            P(None, ("grp", "orb"), None),
            P("orb"),
            P(("grp", "orb")),
            P(("grp", "orb")),
        ),
        out_specs=(
            P(("grp", "orb"), None, None),
            P(None, ("grp", "orb"), None, None),
            P(None, ("grp", "orb"), None),
            P(("grp", "orb")),
        ),
        check_vma=False,
    )
```

```python
import jax
import jax.numpy as jnp
from jax import lax
from jax.experimental import pallas as pl
from jax.experimental.pallas import tpu as pltpu
from jax.sharding import PartitionSpec as P

F32 = jnp.float32
BF16 = jnp.bfloat16
NX, NY, NZ = 4, 4, 8
LAG = 6
VALUE_STEPS = (23, 30, 37)
CHUNK = 16
K = 16
HIGH = lax.Precision.HIGHEST
MESH = pl.DeviceIdType.MESH


def nn(a, b, precision=None):
    return lax.dot_general(
        a, b, (((1,), (0,)), ((), ())), precision=precision, preferred_element_type=F32
    )


def nt(a, b):
    return lax.dot_general(a, b, (((1,), (1,)), ((), ())), preferred_element_type=F32)


def split(a):
    hi = a.astype(BF16)
    return hi, (a - hi.astype(F32)).astype(BF16)


def iota(shape, dim):
    return lax.broadcasted_iota(jnp.int32, shape, dim)


def column(row):
    return jnp.sum(jnp.where(iota((K, K), 0) == iota((K, K), 1), row, 0.0), 1, keepdims=True)


def one_hot(indices, width):
    return jnp.where(iota((K, width), 1) == indices.astype(jnp.int32), 1.0, 0.0)


def pick(hot, row):
    return jnp.sum(hot * row, 1, keepdims=True)


def start(ratio):
    a = augmented(ratio)
    return a, jnp.ones((1, 128), F32), jnp.broadcast_to(a[:, 0:1], a.shape)


def eliminate(state, k):
    a, pivots, col = state
    row = iota(a.shape, 0)
    after = jnp.broadcast_to(a[:, k + 1 : k + 2], a.shape)
    size = jnp.abs(col)
    scaled = size * 257.0
    key = (scaled - (scaled - size)) * (1.0 + row.astype(F32) * 2.0**-22)
    key = jnp.where(row >= k, key, -1.0)
    chosen = key == jnp.max(key, 0, keepdims=True)

    def chosen_row(x):
        return jnp.sum(jnp.where(chosen, x, 0.0), 0, keepdims=True)

    pivot = chosen_row(col)
    factor = jnp.where(chosen, col[k : k + 1], col)
    scale = 1.0 / pivot

    def update(x):
        pivot_row = chosen_row(x) * scale
        return jnp.where(row == k, pivot_row, jnp.where(chosen, x[k : k + 1], x) - factor * pivot_row)

    pivots = jnp.where(iota(pivots.shape, 1) == k, pivot, pivots)
    return update(a), pivots, update(after)


def augmented(x):
    n = x.shape[0]
    r, c = iota(x.shape, 0), iota(x.shape, 1)
    return jnp.where(c < n, x, 0.0) + jnp.where((c == r) | (c == r + n), 1.0, 0.0)


def wave_rows(points, kvec):
    phases = points[0] * kvec[0:1] + points[1] * kvec[1:2]
    phases = phases + points[2] * kvec[2:3]
    return jnp.cos(phases).astype(BF16), jnp.sin(phases).astype(BF16)


def slope_rows(waves, kvec):
    cos, sin = waves[0].astype(F32), waves[1].astype(F32)
    rows = []
    for a in range(3):
        k = kvec[a : a + 1]
        rows.append(((-k * sin).astype(BF16), (k * cos).astype(BF16)))
    square = kvec[0:1] * kvec[0:1] + kvec[1:2] * kvec[1:2] + kvec[2:3] * kvec[2:3]
    rows.append(((-square * cos).astype(BF16), (-square * sin).astype(BF16)))
    return rows


def diagonals(block):
    eye = iota((K, K), 0) == iota((K, K), 1)
    return [
        jnp.sum(jnp.where(eye, block[K * i : K * (i + 1)], 0.0), 0, keepdims=True)
        for i in range(4)
    ]


def main_kernel(
    donor, take, log_weight, kvec_in, pos_in, disp_in, moved_in, coef, inverse,
    chosen, ccat, scat, rest_out,
    mf, mhi, mlo, cbuf, sx, rx, kvec, pk_pos, pk_disp, pk_moved, pk_log, waves, values, cown,
    m_sem, c_sem, y_send, y_recv, p_send, p_recv, x_send, x_recv,
    z_send, z_recv, s_send, s_recv,
):
    ne, ng = mf.shape[0], kvec.shape[1]
    steps = rx.shape[1]
    total = ne // CHUNK
    g = lax.axis_index("grp")
    o = lax.axis_index("orb")
    core, y, z = lax.rem(o, 2), lax.rem(o // 2, NY), o // (2 * NY)

    def orb(zz, yy, cc):
        return (zz * NY + yy) * 2 + cc

    def turn(value, by, size):
        return lax.rem(value + by + size, size)

    def remote(src, dst, send, recv, grp, orb_index):
        return pltpu.make_async_remote_copy(
            src_ref=src, dst_ref=dst, send_sem=send, recv_sem=recv,
            device_id=(grp, orb_index), device_id_type=MESH,
        )

    def shard(zz, yy, cc=core):
        return cbuf.at[zz * NY + yy, cc]

    barrier = pltpu.get_barrier_semaphore()
    up, down = orb(turn(z, 1, NZ), y, core), orb(turn(z, -1, NZ), y, core)
    sibling = orb(z, y, 1 - core)
    partners = [(turn(g, d, NX), o) for d in range(1, NX)]
    partners += [(g, orb(z, turn(y, d, NY), core)) for d in range(1, NY)]
    partners += [(g, up), (g, down), (g, sibling)]
    for partner in partners:
        pl.semaphore_signal(barrier, inc=1, device_id=partner, device_id_type=MESH)

    pieces = m_sem.shape[0]
    piece = ne // pieces
    loads = []
    for i in range(pieces):
        rows = pl.ds(i * piece, piece)
        loads.append(pltpu.make_async_copy(inverse.at[0, rows], mf.at[rows], m_sem.at[i]))
    for i in range(pieces // 2):
        loads[i].start()
        loads[pieces - 1 - i].start()
    small = [
        pltpu.make_async_copy(src, dst, c_sem.at[i])
        for i, (src, dst) in enumerate(
            (
                (kvec_in, kvec),
                (pos_in, pk_pos.at[g]),
                (disp_in, pk_disp.at[g]),
                (moved_in, pk_moved.at[g]),
                (coef, shard(z, y)),
            )
        )
    ]
    for copy in small:
        copy.start()
    pk_log[g] = jnp.full((8, 128), log_weight[0], F32)
    pl.semaphore_wait(barrier, len(partners))

    is_source = donor[0] == g
    right, left = turn(g, 1, NX), turn(g, -1, NX)
    x_copies = {}

    def x_arrived(t):
        for copy in x_copies[t]:
            copy.wait_recv()

    def x_step(t):
        if t >= LAG:
            x_arrived(t - LAG)
        for way, first in ((0, t * CHUNK), (1, ne - (t + 1) * CHUNK)):
            own = mf[first : first + CHUNK].astype(BF16)
            sx[way, t] = jnp.where(is_source, own, rx[way, t - LAG]) if t >= LAG else own
        x_copies[t] = [
            remote(sx.at[way, t], rx.at[way, t], x_send.at[way, t], x_recv.at[way, t], to, o)
            for way, to in ((0, right), (1, left))
        ]
        for copy in x_copies[t]:
            copy.start()

    taking = jnp.logical_and(take[0] == 1, donor[0] != g)
    ahead = lax.rem(g - donor[0] + NX, NX)

    def places_of(r):
        found = []
        for hops in range(1, NX):
            t = r + (hops - 1) * LAG
            if t < steps:
                found.append((0, t))
            else:
                found.append((1, total - 1 - r + (NX - hops - 1) * LAG))
        return found

    ready = {}
    for r in range(total):
        ready.setdefault(max(t for _, t in places_of(r)), []).append(r)

    def select(r):
        rows = pl.ds(r * CHUNK, CHUNK)
        hi, lo = split(mf[rows])
        one, two, three = (rx[way, t] for way, t in places_of(r))
        got = jnp.where(ahead == 1, one, jnp.where(ahead == 2, two, three))
        mhi[rows] = jnp.where(taking, got, hi)
        mlo[rows] = jnp.where(taking, jnp.zeros_like(lo), lo)
        chosen[rows] = jnp.where(taking, got.astype(F32), mf[rows])

    y_copies = [
        remote(coef, shard(z, y), y_send.at[d - 1], y_recv.at[d - 1], g,
               orb(z, turn(y, d, NY), core))
        for d in range(1, NY)
    ]
    laps = NY * (NZ - 1) // 2
    full = NY * (NZ // 2 - 1)
    rest = laps - full
    z_copies, s_copies, seen = {}, {}, set()

    def item(way, k):
        if k < full:
            return k // NY, k % NY
        return NZ // 2 - 1, k - full + (rest if way else 0)

    def place(way, m, j):
        return shard(turn(z, m if way else -m, NZ), turn(y, j, NY))

    def to_sibling(index, src, dst):
        s_copies[index] = remote(src, dst, s_send.at[index], s_recv.at[index], g, sibling)
        s_copies[index].start()

    def z_arrived(way, k):
        if (way, k) not in seen:
            seen.add((way, k))
            z_copies[way, k].wait_recv()
            m, j = item(way, k)
            got = place(way, m + 1, j)
            to_sibling(NY + way * laps + k, got, got)

    def z_step(k):
        if k < laps:
            for way in range(2):
                m, j = item(way, k)
                src = dst = place(way, m, j)
                if m:
                    z_arrived(way, k - NY if k < full else full - NY + j)
                elif j == 0:
                    src = coef
                elif way == 0:
                    y_copies[NY - j - 1].wait_recv()
                z_copies[way, k] = remote(
                    src, dst, z_send.at[way, k], z_recv.at[way, k], g, (up, down)[way]
                )
                z_copies[way, k].start()
                if m == 0 and way == 0:
                    to_sibling(j, src, dst)
        if k >= NY:
            for way in range(2):
                z_arrived(way, k - NY)

    packets = []
    for d in range(1, NX):
        for i, (src, all_slots) in enumerate(
            ((pos_in, pk_pos), (disp_in, pk_disp), (moved_in, pk_moved), (pk_log.at[g], pk_log))
        ):
            packets.append(
                remote(src, all_slots.at[g], p_send.at[d - 1, i], p_recv.at[d - 1, i],
                       turn(g, d, NX), o)
            )
    known = {}

    def find_points():
        for copy in packets:
            copy.wait_recv()
        for copy in small:
            copy.wait()
        parent = jnp.where(taking, donor[0], g)
        hot_own = one_hot(column(pk_moved[g, 0].astype(F32)), ne)
        hot_par = one_hot(column(pk_moved[parent, 0].astype(F32)), ne)
        hot_next = one_hot(column(pk_moved[g, 1].astype(F32)), ne)
        old_own = [pick(hot_own, pk_pos[g, a]) for a in range(3)]
        new_own = [old_own[a] + column(pk_disp[g, a]) for a in range(3)]
        old_par = [pick(hot_par, pk_pos[parent, a]) for a in range(3)]
        new_par = [old_par[a] + column(pk_disp[parent, a]) for a in range(3)]
        was_moved = jnp.sum(hot_par, 0, keepdims=True) > 0.0
        old_next = []
        for a in range(3):
            placed = jnp.sum(hot_par * new_par[a], 0, keepdims=True)
            old_next.append(pick(hot_next, jnp.where(was_moved, placed, pk_pos[parent, a])))
        new_next = [old_next[a] + column(pk_disp[g, 3 + a]) for a in range(3)]
        known["points"] = (old_own, old_par, new_par, old_next, new_own, new_next)
        zeros = jnp.zeros((2 * K, ne), F32)
        pair = jnp.concatenate([hot_par, hot_next], 0)
        known["hi"] = jnp.concatenate([pair, zeros, pair, zeros], 0).astype(BF16)
        known["lo"] = jnp.concatenate([zeros, pair, zeros, zeros], 0).astype(BF16)
        wide = jnp.zeros((128 - 2 * K, ne), F32)
        none = jnp.zeros((K, ne), F32)
        known["own_hi"] = jnp.concatenate([hot_own, none, wide], 0).astype(BF16)
        known["own_lo"] = jnp.concatenate([none, hot_own, wide], 0).astype(BF16)
        known["log"] = pk_log[parent]

    def find_waves(i):
        pair = wave_rows(known["points"][i], kvec[...])
        first = i * K if i < 4 else 4 * K + (i - 4) * 5 * K
        rows = [pair] + (slope_rows(pair, kvec[...]) if i >= 4 else [])
        for n, (cos, sin) in enumerate(rows):
            waves[first + n * K : first + (n + 1) * K, :ng] = cos
            waves[first + n * K : first + (n + 1) * K, ng:] = sin

    block = 2 * NY * K

    def find_values(m):
        ends = [turn(z, m + 1, NZ), turn(z, -m, NZ)]
        table = jnp.concatenate(
            [cbuf[pl.ds(e * NY, NY)].reshape(block, cbuf.shape[3]) for e in ends], 0
        )
        result = nt(waves[...], table)
        for i, e in enumerate(ends):
            lanes = pl.ds(pl.multiple_of(e * block, block), block)
            values[:, lanes] = result[:, i * block : (i + 1) * block]

    def s_wait(m):
        for way in range(2):
            for k in range(laps):
                offset = item(way, k)[0] + 1
                if offset == (m + 1 if way else m) or offset == m + 1 == NZ // 2:
                    s_copies[NY + way * laps + k].wait_recv()
        if m == 0:
            for j in range(NY):
                s_copies[j].wait_recv()

    tile = min(256, ne)

    def own_columns(i):
        rows = pl.ds(i * tile, tile)
        hi, lo = split(mf[rows])
        cown[rows] = (nt(hi, known["own_hi"]) + nt(lo, known["own_lo"])).astype(BF16)

    def columns(i):
        rows = pl.ds(i * tile, tile)
        ccat[rows] = (nt(mhi[rows], known["hi"]) + nt(mlo[rows], known["lo"])).astype(BF16)

    tiles = ne // tile
    work = {}

    def plan(t, what, *args):
        work.setdefault(min(t, steps - 1), []).append((what, args))

    plan(8, find_points)
    for i in range(6):
        plan(9 + i, find_waves, i)
    for i in range(tiles):
        plan(15 + i, own_columns, i)
    early = [i for i in (0, tiles - 1) if tiles > 2]
    for i in early:
        plan(steps - 3 + (i > 0), columns, i)
    for m in range(NZ // 2 - 1):
        plan(VALUE_STEPS[m], lambda m: (s_wait(m), find_values(m)), m)

    for t in range(steps):
        for i in range(pieces // 2):
            if t == 2 * i:
                loads[i].wait()
                loads[pieces - 1 - i].wait()
        x_step(t)
        if t == 0:
            for copy in y_copies + packets:
                copy.start()
        if t >= LAG:
            for r in ready.get(t - LAG, ()):
                select(r)
        for k in range(laps + NY):
            if t == (min(2 * k + 4, steps - 1) if k else 0):
                z_step(k)
        for what, args in work.get(t, ()):
            what(*args)
    s_wait(NZ // 2 - 1)
    find_values(NZ // 2 - 1)

    def stacked(rows):
        hi, lo = split(rows)
        return jnp.concatenate([hi, lo], 0)

    base, second = 4 * K, 9 * K
    own_left = stacked(
        jnp.concatenate([values[base : base + K] - values[0:K], values[base + K : second]], 0)
    )
    changes = jnp.concatenate(
        [values[2 * K : 3 * K] - values[K : 2 * K], values[second : second + K] - values[3 * K : base]], 0
    )
    slopes = values[second + K :]
    left = stacked(jnp.concatenate([changes, slopes], 0))
    cut = own_left.shape[0] // 2
    own_got = nn(own_left, cown[...])
    own_g = own_got[:cut] + own_got[cut:]
    own_g = own_g[:, :K] + own_got[:cut, K : 2 * K]
    for t in range(steps - LAG, steps):
        x_arrived(t)
        for r in ready.get(t, ()):
            select(r)
    for i in range(tiles):
        if i not in early:
            columns(i)
    cut = left.shape[0] // 2
    got = nn(left, ccat[...])
    lanes = got[:cut] + got[cut:]
    ratio_g = lanes[:, : 2 * K] + got[:cut, 2 * K : 4 * K]

    def widen(x):
        return jnp.concatenate([x, jnp.zeros((x.shape[0], 128 - x.shape[1]), F32)], 1)

    state = start(widen(ratio_g[: 2 * K]))
    for k in range(2 * K):
        state = eliminate(state, k)
    inverse_32 = state[0][:, 2 * K : 4 * K]
    change_hi, change_lo = split(changes)
    change_both = jnp.concatenate([change_hi, change_lo], 0)
    product = nn(change_both, mhi[...])
    product = product[: 2 * K] + product[2 * K :] + nn(change_hi, mlo[...])
    product_hi, product_lo = split(product)
    inverse_both = stacked(inverse_32)
    solved = nn(inverse_both, product_hi)
    solved = solved[: 2 * K] + solved[2 * K :] + nn(inverse_both[: 2 * K], product_lo)
    solved_hi, solved_lo = split(solved)
    scat[...] = jnp.concatenate(
        [solved_hi, solved_hi, solved_lo, jnp.zeros((2 * K, ne), BF16)], 0
    )
    rest_out[0 : 5 * K] = widen(own_g)
    rest_out[5 * K : 9 * K] = widen(ratio_g[2 * K :])
    rest_out[9 * K : 11 * K] = widen(inverse_32)
    rest_out[11 * K : 11 * K + 8] = jnp.broadcast_to(state[1], (8, 128))
    rest_out[11 * K + 8 :] = known["log"]

    for copy in y_copies + packets + list(z_copies.values()) + list(s_copies.values()):
        copy.wait_send()
    for copies in x_copies.values():
        for copy in copies:
            copy.wait_send()


def finish_kernel(chosen, ccat, scat, rest_in, out, drift, lap, weight, rows_f, sems):
    parts = sems.shape[0]
    size = chosen.shape[0] // parts
    copies = []
    for i in range(parts):
        rows = pl.ds(i * size, size)
        rows_f[rows] = chosen[rows] - nn(ccat[rows], scat[...])
        copies.append(pltpu.make_async_copy(rows_f.at[rows], out.at[0, rows], sems.at[i]))
        copies[-1].start()
    own_state = start(rest_in[0:K])
    for k in range(K):
        own_state = eliminate(own_state, k)
    own_inverse = own_state[0][:, K : 2 * K]
    inverse_32 = rest_in[9 * K : 11 * K, : 2 * K]
    first = diagonals(nn(rest_in[K : 5 * K, :K], own_inverse, HIGH))
    second = diagonals(nn(rest_in[5 * K : 9 * K, : 2 * K], inverse_32[:, K:], HIGH))
    for update, rows in enumerate((first, second)):
        for a in range(3):
            drift[3 * update + a] = rows[a]
        lap[update] = rows[3]
    logs = jnp.sum(jnp.log(jnp.abs(rest_in[11 * K : 11 * K + 1])), 1, keepdims=True)
    weight[...] = rest_in[11 * K + 8 : 11 * K + 9, 0:1] + logs
    for copy in copies:
        copy.wait()


def per_device(
    wavevectors, coefficients, inverse, positions, displacements, moved, donor, take, log_weight
):
    ne = inverse.shape[1]
    npw = coefficients.shape[0]
    ng = wavevectors.shape[1]
    steps = ne // 2 // CHUNK + LAG
    laps = NY * (NZ - 1) // 2
    vmem = pl.BlockSpec(memory_space=pltpu.VMEM)
    smem = pl.BlockSpec(memory_space=pltpu.SMEM)
    hbm = pl.BlockSpec(memory_space=pltpu.HBM)
    dma = pltpu.SemaphoreType.DMA
    shape = jax.ShapeDtypeStruct
    smalls = (shape((6, 1, K), F32), shape((2, 1, K), F32), shape((1, 1), F32))
    states = pl.pallas_call(
        main_kernel,
        out_shape=(
            shape((ne, ne), F32),
            shape((ne, 128), BF16),
            shape((128, ne), BF16),
            shape((12 * K, 128), F32),
        ),
        in_specs=[smem] * 3 + [hbm] * 6,
        out_specs=(vmem,) * 4,
        scratch_shapes=[
            pltpu.VMEM((ne, ne), F32),
            pltpu.VMEM((ne, ne), BF16),
            pltpu.VMEM((ne, ne), BF16),
            pltpu.VMEM((NZ * NY, 2, K, npw), BF16),
            pltpu.VMEM((2, steps, CHUNK, ne), BF16),
            pltpu.VMEM((2, steps, CHUNK, ne), BF16),
            pltpu.VMEM((3, ng), F32),
            pltpu.VMEM((NX, 3, 1, ne), F32),
            pltpu.VMEM((NX, 6, 1, K), F32),
            pltpu.VMEM((NX, 2, 1, K), jnp.int32),
            pltpu.VMEM((NX, 8, 128), F32),
            pltpu.VMEM((14 * K, npw), BF16),
            pltpu.VMEM((14 * K, ne), F32),
            pltpu.VMEM((ne, 128), BF16),
            dma((8,)),
            dma((5,)),
            dma((NY - 1,)),
            dma((NY - 1,)),
            dma((NX - 1, 4)),
            dma((NX - 1, 4)),
            dma((2, steps)),
            dma((2, steps)),
            dma((2, laps)),
            dma((2, laps)),
            dma((NY + 2 * laps,)),
            dma((NY + 2 * laps,)),
        ],
        compiler_params=pltpu.CompilerParams(
            collective_id=0, has_side_effects=True, vmem_limit_bytes=40 << 20
        ),
        name="exchange_and_update",
    )(
        donor,
        take,
        log_weight,
        *(
            pltpu.with_memory_space_constraint(x, pltpu.HBM)
            for x in (
                wavevectors,
                positions.transpose(1, 0, 2),
                displacements.reshape(6, 1, K),
                moved,
                coefficients.T,
                inverse,
            )
        ),
    )
    result, drift, lap, weight = pl.pallas_call(
        finish_kernel,
        out_shape=(shape((1, ne, ne), F32),) + smalls,
        in_specs=[vmem] * 4,
        out_specs=(hbm,) + (vmem,) * 3,
        scratch_shapes=[pltpu.VMEM((ne, ne), F32), dma((8,))],
        compiler_params=pltpu.CompilerParams(vmem_limit_bytes=16 << 20),
        name="rank_update",
    )(*states)
    return (result, drift.reshape(2, 1, 3, K), lap, weight.reshape(1))


def solution(mesh):
    return jax.shard_map(
        per_device,
        mesh=mesh,
        in_specs=(
            P(),
            P(None, "orb"),
            P(("grp", "orb"), None, None),
            P(("grp", "orb"), None, None),
            P(None, ("grp", "orb"), None, None),
            P(None, ("grp", "orb"), None),
            P("orb"),
            P(("grp", "orb")),
            P(("grp", "orb")),
        ),
        out_specs=(
            P(("grp", "orb"), None, None),
            P(None, ("grp", "orb"), None, None),
            P(None, ("grp", "orb"), None),
            P(("grp", "orb")),
        ),
        check_vma=False,
    )
```
